32 devices in a mesh: grp: 2 (over y), band: 8 (over z, x), filt: 2 (over core).
Axes of the slice: x: 2, y: 2, z: 4, core: 2. Of those that a mesh axis runs over, the one named last changes fastest.
Arguments:
- coeff_maps: bfloat16 [128, 64, 512], P(('grp', 'filt'), 'band'), parts along dimension 0, may hold values from -0.75 to 0.75
- image: bfloat16 [6, 64, 512], P('grp', 'band'), parts along dimension 0, may hold values from -24 to 24
- target: bfloat16 [1024, 2, 3, 64, 64], P(('grp', 'band'), None, None, 'filt'), parts along dimension 0, may hold values from -1.5 to 1.5
- dual_rim: float32 [128, 768], P(('grp', 'filt')), parts along dimension 0, may hold values from -18 to 18, as said below
Outputs:
- dict_spectra: bfloat16 [1024, 2, 3, 64, 64], P(('grp', 'band'), None, None, 'filt'), parts along dimension 0
- dictionary: float32 [128, 768], P(('grp', 'filt')), parts along dimension 0
The draws below stay inside these ranges and needn't reach their ends.
There are 2 independent parts, one for each index of `grp`. The reference program is written for one: setup_inputs(seed, part) draws one part's arguments, and reference() takes and returns one part's arrays. A program takes and returns all parts, laid end to end along the dimension named above; each array names one. Nothing has to cross between parts.
Inputs may be any that keep to these rules, and one draw needn't show every extreme that they name: `dual_rim`: a scaled dual variable on the filters' support.
All inputs are finite; a program needn't handle non-finite values.
Results may differ from the reference program's by a relative error of at most 0.0059.
Values may be sent and summed in bfloat16 or wider, within the bound.
No kernel may reach another device: no remote copies, remote signals or barrier semaphores. Data moves between devices by JAX's collectives and lax.ppermute only.
A program may use at most 128 MiB of HBM per device.

```python
import math
import jax
import jax.numpy as jnp
from jax import lax

M = 64
C = 3
K = 16
N = 512
H = 64
N_BAND = 8


def draw_dual_rim(key, part):
    key_scale, key_base = jax.random.split(key)
    scales = jnp.exp(jax.random.uniform(key_scale, (M, 1), jnp.float32, math.log(0.1), math.log(3.0)))
    base = jnp.clip(jax.random.normal(key_base, (M, C * K * K), jnp.float32), -6.0, 6.0)
    return base * scales


def level_of(stream_key, shape, pieces, least, largest):
    def one(dim, parts):
        draws = jax.random.uniform(jax.random.fold_in(jax.random.fold_in(stream_key, 6), dim), (parts,), jnp.float32, least / len(pieces), largest / len(pieces))
        return jnp.repeat(jnp.exp(draws), shape[dim] // parts).reshape((-1,) + (1,) * (len(shape) - dim - 1))

    level = one(*pieces[0])
    for cut in pieces[1:]:
        level = level * one(*cut)
    return level


def bell_draw(stream_key, shape, scale, limit, cuts=(), held_as=jnp.bfloat16):
    values = scale * jax.random.normal(stream_key, shape, jnp.float32)
    if cuts:
        values = values * level_of(stream_key, shape, cuts, -0.22, 0.18)
    return jnp.clip(values, -limit, limit).astype(held_as)


def setup_inputs(seed: int = 0, part: int = 0) -> dict:
    seeds = jax.random.split(jax.random.key(seed), 5)
    part_keys = jax.random.split(jax.random.fold_in(seeds[4], part), 5)
    return {
        "coeff_maps": bell_draw(part_keys[0], (M, H, N), 0.125, 0.75, ((0, 2), (1, 8))),
        "image": bell_draw(part_keys[1], (C, H, N), 4.0, 24.0, ((1, 8),)),
        "target": bell_draw(part_keys[2], (N, 2, C, M, H), 0.25, 1.5, ((0, 8), (3, 2))),
        "dual_rim": draw_dual_rim(jax.random.fold_in(jax.random.fold_in(seeds[4], part), 71), part),
    }


penalty = 1.0

def forward_columns(length):
    ramp = jnp.arange(length, dtype=jnp.int32)
    phases = ramp[:, None] * ramp[None, :] % length
    angles = phases.astype(jnp.float32) * (2.0 * math.pi / length)
    factor = 1.0 / math.sqrt(length)
    lookup = jnp.stack([jnp.cos(angles) * factor, -jnp.sin(angles) * factor], axis=2)
    return lookup.reshape(length, 2 * length).astype(jnp.bfloat16)

def forward_rows(length):
    ramp = jnp.arange(length, dtype=jnp.int32)
    phases = ramp[:, None] * ramp[None, :] % length
    angles = phases.astype(jnp.float32) * (2.0 * math.pi / length)
    factor = 1.0 / math.sqrt(length)
    return jnp.stack([jnp.cos(angles) * factor, jnp.sin(angles) * factor], axis=0).astype(jnp.bfloat16)

def inverse_rows(length, width):
    ramp = jnp.arange(length, dtype=jnp.int32)
    reach = jnp.arange(width, dtype=jnp.int32)
    phases = ramp[:, None] * reach[None, :] % length
    angles = phases.astype(jnp.float32) * (2.0 * math.pi / length)
    factor = 1.0 / math.sqrt(length)
    return jnp.stack([jnp.cos(angles) * factor, jnp.sin(angles) * factor], axis=1)

def inverse_columns(offset, length, total_cols, width):
    freqs = offset + jnp.arange(length, dtype=jnp.int32)
    reach = jnp.arange(width, dtype=jnp.int32)
    phases = freqs[:, None] * reach[None, :] % total_cols
    angles = phases.astype(jnp.float32) * (2.0 * math.pi / total_cols)
    factor = 1.0 / math.sqrt(total_cols)
    return jnp.stack([jnp.cos(angles) * factor, jnp.sin(angles) * factor], axis=1)

def spectra(slab_rows, lookup, freqs, members):
    height = slab_rows.shape[0]
    products = jnp.einsum('hk,tgh->ktg', slab_rows.astype(jnp.float32), lookup.astype(jnp.float32), precision=lax.Precision.HIGHEST)
    products = products.reshape(freqs, 2, members, 2, height)
    real_part = products[:, 0, :, 0] + products[:, 1, :, 1]
    imag_part = products[:, 1, :, 0] - products[:, 0, :, 1]
    return (real_part, imag_part)

def reference(coeff_maps, image, target, dual_rim):
    per_band = N // N_BAND
    slab_count = N_BAND
    col_lookup = forward_columns(N)
    row_lookup = forward_rows(H)
    rim_lookup = inverse_rows(H, K)
    col_maps = jnp.dot(coeff_maps.reshape(M * H, N), col_lookup, preferred_element_type=jnp.float32)
    col_maps = col_maps.astype(jnp.bfloat16).reshape(M, H, N, 2).transpose(1, 2, 3, 0)
    col_maps = col_maps.reshape(H, slab_count, per_band * 2 * M).transpose(1, 0, 2)
    col_image = jnp.dot(image.reshape(C * H, N), col_lookup, preferred_element_type=jnp.float32)
    col_image = col_image.astype(jnp.bfloat16).reshape(C, H, N, 2).transpose(1, 2, 3, 0)
    col_image = col_image.reshape(H, slab_count, per_band * 2 * C).transpose(1, 0, 2)
    target_slabs = target.reshape(slab_count, per_band, 2, C, M, H)
    slab_ids = jnp.arange(slab_count, dtype=jnp.int32)

    def step_fn(carried, inputs):
        maps_slab, image_slab, target_slab, slab_id = inputs
        x_re, x_im = spectra(maps_slab, row_lookup, per_band, M)
        s_re, s_im = spectra(image_slab, row_lookup, per_band, C)
        v_full = target_slab.astype(jnp.float32)
        v_re = v_full[:, 0]
        v_im = v_full[:, 1]
        energy = lax.optimization_barrier(jnp.sum(x_re * x_re + x_im * x_im, axis=1))
        cross_re = lax.optimization_barrier(jnp.sum(x_re[:, None] * v_re - x_im[:, None] * v_im, axis=2))
        cross_im = lax.optimization_barrier(jnp.sum(x_re[:, None] * v_im + x_im[:, None] * v_re, axis=2))
        denom = penalty + energy[:, None, :]
        coef_re = (s_re - cross_re) / denom
        coef_im = (s_im - cross_im) / denom
        dict_real = v_re + x_re[:, None] * coef_re[:, :, None] + x_im[:, None] * coef_im[:, :, None]
        dict_imag = v_im + x_re[:, None] * coef_im[:, :, None] - x_im[:, None] * coef_re[:, :, None]
        dict_full = jnp.stack([dict_real, dict_imag], axis=1)
        folded = jnp.einsum('qpcmg,gty->qpcmty', dict_full, rim_lookup, precision=lax.Precision.HIGHEST)
        rim_real = folded[:, 0, :, :, 0] - folded[:, 1, :, :, 1]
        rim_imag = folded[:, 0, :, :, 1] + folded[:, 1, :, :, 0]
        lookup = inverse_columns(slab_id * per_band, per_band, N, K)
        carried = carried + jnp.einsum('qcmy,qx->mcyx', rim_real, lookup[:, 0], precision=lax.Precision.HIGHEST)
        carried = carried - jnp.einsum('qcmy,qx->mcyx', rim_imag, lookup[:, 1], precision=lax.Precision.HIGHEST)
        return (carried, dict_full.astype(jnp.bfloat16))
    start_sum = jnp.zeros((M, C, K, K), jnp.float32)
    spatial, dict_slabs = lax.scan(step_fn, start_sum, (col_maps, col_image, target_slabs, slab_ids))
    dict_spectra = dict_slabs.reshape(N, 2, C, M, H)
    joined = spatial.reshape(M, C * K * K) + dual_rim
    spread = jnp.sqrt(lax.optimization_barrier(jnp.mean(joined * joined, axis=1, keepdims=True)))
    dictionary = joined / jnp.maximum(spread, 1.0)
    return (dict_spectra, dictionary)
```

```python
import math

import jax
import jax.numpy as jnp
import numpy as np
from jax import lax
from jax.experimental import pallas as pl
from jax.experimental.pallas import tpu as pltpu
from jax.sharding import PartitionSpec as P

K = 16
LANES = 128
HALF = 64

penalty = 1.0

bf16 = jnp.bfloat16
f32 = jnp.float32


def column_table(length, bands):
    ramp = np.arange(length)
    angles = (ramp[:, None] * ramp[None, :] % length) * (2.0 * math.pi / length)
    factor = 1.0 / math.sqrt(length)
    table = np.stack([np.cos(angles) * factor, -np.sin(angles) * factor], axis=1)
    table = table.reshape(length, 2, bands, length // bands).transpose(0, 2, 1, 3)
    return table.reshape(length, 2 * length).astype(np.float32).astype(bf16)


def row_table(height, band_rows):
    ramp = np.arange(height)
    angles = (ramp[:, None] * ramp[None, :] % height) * (2.0 * math.pi / height)
    factor = 1.0 / math.sqrt(height)
    cos, sin = np.cos(angles) * factor, np.sin(angles) * factor
    both = np.stack(
        [np.concatenate([cos, -sin], axis=1), np.concatenate([sin, cos], axis=1)]
    )
    both = both.reshape(2, height // band_rows, band_rows, 2 * height)
    table = np.zeros((2, height // band_rows, 2, band_rows, 2, 2 * height))
    table[:, :, 0, :, 0] = both
    table[:, :, 1, :, 1] = both
    return table.reshape(4 * height, 4 * height).astype(np.float32).astype(bf16)


def angle_tables(height, columns, width):
    reach = np.arange(width)
    rows = (np.arange(height)[:, None] * reach[None, :] % height) * (2.0 * math.pi / height)
    rows = np.repeat(rows, width, axis=1)
    cols = (np.arange(columns)[:, None] * reach[None, :] % columns) * (2.0 * math.pi / columns)
    cols = np.tile(cols, (1, width))
    factor = 1.0 / math.sqrt(height * columns)
    row_pair = np.stack([np.cos(rows) * factor, np.sin(rows) * factor])
    col_pair = np.stack([np.cos(cols), np.sin(cols)])
    return row_pair.astype(np.float32), col_pair.astype(np.float32)


def low_lanes(shape):
    return lax.broadcasted_iota(jnp.int32, shape, len(shape) - 1) < HALF


def columns_kernel(maps_ref, image_ref, table_ref, out_ref):
    bands = out_ref.shape[0]
    rows = maps_ref.shape[0]
    for b in range(bands):
        table = table_ref[:, b * LANES : (b + 1) * LANES]
        out_ref[b, :rows] = jnp.dot(maps_ref[...], table, preferred_element_type=f32).astype(bf16)
        out_ref[b, rows:] = jnp.dot(image_ref[...], table, preferred_element_type=f32).astype(bf16)


def prepare_kernel(target_ref, row_ref, col_ref, packed_ref, inverse_ref):
    freqs, _, channels, filters, height = target_ref.shape

    def step(q, carry):
        for c in range(channels):
            packed_ref[q, c] = jnp.concatenate(
                [target_ref[q, 0, c].astype(f32), target_ref[q, 1, c].astype(f32)], axis=-1
            )
        cos_col = col_ref[0, pl.ds(q, 1), :]
        sin_col = col_ref[1, pl.ds(q, 1), :]
        cos_row = row_ref[0]
        sin_row = row_ref[1]
        inverse_ref[q, :height] = (cos_row * cos_col - sin_row * sin_col).astype(bf16)
        inverse_ref[q, height:] = (-(sin_row * cos_col) - cos_row * sin_col).astype(bf16)
        return carry

    lax.fori_loop(0, freqs, step, 0, unroll=2)


def rows_kernel(got_ref, table_ref, packed_ref, x_ref, image_ref, own_ref, send_ref, one_ref, two_ref):
    freqs, channels, filters, _ = packed_ref.shape
    sources, rows, _ = got_ref.shape
    band_rows = rows // (filters + channels)
    pair = 2 * band_rows
    table = table_ref[...]

    def transform(start):
        block = got_ref[:, start : start + pair, :].reshape(sources * pair, LANES)
        turned = block.T
        left = jnp.concatenate([turned[:freqs], turned[freqs:]], axis=1)
        return jnp.dot(left, table, preferred_element_type=f32)

    for j in range(filters // 2):
        both = transform(j * pair)
        x_ref[pl.ds(2 * j, freqs, stride=filters), :] = both[:, :LANES]
        x_ref[pl.ds(2 * j + 1, freqs, stride=filters), :] = both[:, LANES:]
    for c in range(channels):
        first = min(c, channels - 2)
        both = transform((filters + first) * band_rows)
        part = (c - first) * LANES
        image_ref[c * freqs : (c + 1) * freqs, :] = both[:, part : part + LANES]

    group = 8

    def step(i, carry):
        q0 = pl.multiple_of(i * group, group)
        x = x_ref[pl.ds(pl.multiple_of(q0 * filters, group * filters), group * filters), :]
        y = pltpu.roll(x, HALF, 1)
        x = x.reshape(group, filters, LANES)
        y = y.reshape(group, filters, LANES)
        one_ref[pl.ds(channels * freqs + q0, group), :] = jnp.sum(x * x, axis=1)
        for c in range(channels):
            v = packed_ref[pl.ds(q0, group), c]
            one_ref[pl.ds(c * freqs + q0, group), :] = jnp.sum(x * v, axis=1)
            two_ref[pl.ds(c * freqs + q0, group), :] = jnp.sum(y * v, axis=1)
        return carry

    lax.fori_loop(0, freqs // group, step, 0)
    top = channels * freqs
    one = one_ref[:top]
    two = two_ref[...]
    low = low_lanes(one.shape)
    cross = jnp.where(low, one - pltpu.roll(one, HALF, 1), two + pltpu.roll(two, HALF, 1))
    energy = one_ref[top:]
    energy = energy + pltpu.roll(energy, HALF, 1)
    own_ref[:top] = cross
    own_ref[top:] = energy
    send_ref[:top] = cross.astype(bf16)
    send_ref[top:] = energy.astype(bf16)


def solve_kernel(
    x_ref, packed_ref, image_ref, own_ref, peer_ref, inverse_ref, out_ref, rim_ref, re_ref, im_ref
):
    freqs, channels, filters, _ = packed_ref.shape
    top = channels * freqs
    total = own_ref[...] + peer_ref[...].astype(f32)
    denom = penalty + total[top:]
    low = low_lanes(denom.shape)
    for c in range(channels):
        span = slice(c * freqs, (c + 1) * freqs)
        coef = (image_ref[span] - total[span]) / denom
        turned = pltpu.roll(coef, HALF, 1)
        re_ref[span] = jnp.where(low, coef, -turned)
        im_ref[span] = jnp.where(low, turned, coef)

    def step(i, acc):
        sides = []
        for k in range(2):
            q = 2 * i + k
            x = x_ref[pl.ds(pl.multiple_of(q * filters, filters), filters), :]
            y = pltpu.roll(x, HALF, 1)
            parts = []
            for c in range(channels):
                d = (
                    packed_ref[q, c]
                    + x * re_ref[pl.ds(c * freqs + q, 1), :]
                    + y * im_ref[pl.ds(c * freqs + q, 1), :]
                )
                d = d.astype(bf16)
                out_ref[q, 0, c] = d[:, :HALF]
                out_ref[q, 1, c] = d[:, HALF:]
                parts.append(d)
            sides.append(jnp.concatenate(parts, axis=0))
        left = jnp.concatenate(sides, axis=1)
        right = inverse_ref[pl.ds(2 * i, 2)].reshape(2 * LANES, inverse_ref.shape[2])
        return acc + jnp.dot(left, right, preferred_element_type=f32)

    acc = jnp.zeros(rim_ref.shape, f32)
    acc = lax.fori_loop(0, freqs // 2, step, acc, unroll=2)
    rim_ref[...] = acc.astype(bf16)


def finish_kernel(*refs):
    part_refs, dual_ref, out_ref = refs[:-2], refs[-2], refs[-1]
    filters = dual_ref.shape[0]
    sums = [r[...].astype(f32) for r in part_refs]
    while len(sums) > 1:
        sums = [sums[i] + sums[i + 1] for i in range(0, len(sums), 2)]
    area = sums[0].shape[1]
    channels = sums[0].shape[0] // filters
    joined = [
        sums[0][c * filters : (c + 1) * filters] + dual_ref[:, c * area : (c + 1) * area]
        for c in range(channels)
    ]
    squares = sum(jnp.sum(w * w, axis=1, keepdims=True) for w in joined)
    spread = jnp.sqrt(squares / (channels * area))
    scale = jnp.maximum(spread, 1.0)
    for c in range(channels):
        out_ref[:, c * area : (c + 1) * area] = joined[c] / scale


def params():
    return pltpu.CompilerParams(vmem_limit_bytes=48 * 1024 * 1024)


def plain(coeff_maps, image, target, dual_rim):
    filters, band_rows, width_cols = coeff_maps.shape
    channels = image.shape[0]
    bands = lax.axis_size("band")
    height = band_rows * bands
    freqs = width_cols // bands
    table = jnp.asarray(column_table(width_cols, bands)).reshape(width_cols, bands, 2 * freqs)
    stacked = jnp.concatenate([coeff_maps, image], axis=0)
    send = jnp.einsum("mrn,nbk->brmk", stacked, table, preferred_element_type=f32)
    got = lax.all_to_all(send.astype(bf16), "band", split_axis=0, concat_axis=0)
    got = got.reshape(height, filters + channels, 2, freqs)
    ramp = jnp.arange(height, dtype=jnp.int32)
    angles = (ramp[:, None] * ramp[None, :] % height).astype(f32) * (2.0 * math.pi / height)
    factor = 1.0 / math.sqrt(height)
    lookup = jnp.stack([jnp.cos(angles) * factor, jnp.sin(angles) * factor]).astype(bf16)
    both = jnp.einsum("hmpq,tgh->ptqmg", got, lookup, preferred_element_type=f32)
    re = both[0, 0] + both[1, 1]
    im = both[1, 0] - both[0, 1]
    x_re, s_re = re[:, :filters], re[:, filters:]
    x_im, s_im = im[:, :filters], im[:, filters:]
    v_re = target[:, 0].astype(f32)
    v_im = target[:, 1].astype(f32)
    energy = jnp.sum(x_re * x_re + x_im * x_im, axis=1)
    cross_re = jnp.sum(x_re[:, None] * v_re - x_im[:, None] * v_im, axis=2)
    cross_im = jnp.sum(x_re[:, None] * v_im + x_im[:, None] * v_re, axis=2)
    sums = jnp.concatenate([cross_re, cross_im, energy[:, None]], axis=1)
    sums = lax.psum(sums.astype(bf16), "filt").astype(f32)
    denom = penalty + sums[:, 2 * channels :]
    coef_re = ((s_re - sums[:, :channels]) / denom)[:, :, None]
    coef_im = ((s_im - sums[:, channels : 2 * channels]) / denom)[:, :, None]
    d_re = v_re + x_re[:, None] * coef_re + x_im[:, None] * coef_im
    d_im = v_im + x_re[:, None] * coef_im - x_im[:, None] * coef_re
    reach = jnp.arange(K, dtype=jnp.int32)
    rows = (ramp[:, None] * reach[None, :] % height).astype(f32) * (2.0 * math.pi / height)
    cols = lax.axis_index("band") * freqs + jnp.arange(freqs, dtype=jnp.int32)
    cols = (cols[:, None] * reach[None, :] % width_cols).astype(f32) * (2.0 * math.pi / width_cols)
    turn = rows[None, :, :, None] + cols[:, None, None, :]
    factor = 1.0 / math.sqrt(height * width_cols)
    exact = lax.Precision.HIGHEST
    spatial = jnp.einsum("qcmg,qgyx->mcyx", d_re, jnp.cos(turn) * factor, precision=exact)
    spatial -= jnp.einsum("qcmg,qgyx->mcyx", d_im, jnp.sin(turn) * factor, precision=exact)
    spatial = lax.psum(spatial.reshape(dual_rim.shape), "band")
    joined = spatial + dual_rim
    spread = jnp.sqrt(jnp.mean(joined * joined, axis=1, keepdims=True))
    dict_spectra = jnp.stack([d_re, d_im], axis=1).astype(bf16)
    return (dict_spectra, joined / jnp.maximum(spread, 1.0))


def body(coeff_maps, image, target, dual_rim):
    filters, band_rows, width_cols = coeff_maps.shape
    channels = image.shape[0]
    bands = lax.axis_size("band")
    height = band_rows * bands
    freqs = width_cols // bands
    rows = (filters + channels) * band_rows
    if (2 * freqs, 2 * height, 16 % band_rows, filters % 2, bands & (bands - 1)) != (LANES, LANES, 0, 0, 0):
        return plain(coeff_maps, image, target, dual_rim)

    send = pl.pallas_call(
        columns_kernel,
        out_shape=jax.ShapeDtypeStruct((bands, rows, LANES), bf16),
        compiler_params=params(),
        name="columns",
    )(
        coeff_maps.reshape(filters * band_rows, width_cols),
        image.reshape(channels * band_rows, width_cols),
        jnp.asarray(column_table(width_cols, bands)),
    )
    got = lax.all_to_all(send, "band", split_axis=0, concat_axis=0)

    row_pair, col_pair = angle_tables(height, width_cols, K)
    first = lax.axis_index("band") * freqs
    col_mine = lax.dynamic_slice_in_dim(jnp.asarray(col_pair), first, freqs, axis=1)
    packed, inverse = pl.pallas_call(
        prepare_kernel,
        out_shape=(
            jax.ShapeDtypeStruct((freqs, channels, filters, LANES), f32),
            jax.ShapeDtypeStruct((freqs, LANES, K * K), bf16),
        ),
        compiler_params=params(),
        name="prepare",
    )(target, jnp.asarray(row_pair), col_mine)

    lines = (channels + 1) * freqs
    x, lit, own, sums = pl.pallas_call(
        rows_kernel,
        out_shape=(
            jax.ShapeDtypeStruct((freqs * filters, LANES), f32),
            jax.ShapeDtypeStruct((channels * freqs, LANES), f32),
            jax.ShapeDtypeStruct((lines, LANES), f32),
            jax.ShapeDtypeStruct((lines, LANES), bf16),
        ),
        scratch_shapes=[
            pltpu.VMEM((lines, LANES), f32),
            pltpu.VMEM((channels * freqs, LANES), f32),
        ],
        compiler_params=params(),
        name="rows",
    )(got, jnp.asarray(row_table(height, band_rows)), packed)

    peer = lax.ppermute(sums, "filt", [(0, 1), (1, 0)])

    dict_spectra, rim = pl.pallas_call(
        solve_kernel,
        out_shape=(
            jax.ShapeDtypeStruct(target.shape, bf16),
            jax.ShapeDtypeStruct((channels * filters, K * K), bf16),
        ),
        scratch_shapes=[
            pltpu.VMEM((channels * freqs, LANES), f32),
            pltpu.VMEM((channels * freqs, LANES), f32),
        ],
        compiler_params=params(),
        name="solve",
    )(x, packed, lit, own, peer, inverse)

    parts = [rim] + [
        lax.ppermute(rim, "band", [(i, i ^ k) for i in range(bands)]) for k in range(1, bands)
    ]
    dictionary = pl.pallas_call(
        finish_kernel,
        out_shape=jax.ShapeDtypeStruct(dual_rim.shape, f32),
        compiler_params=params(),
        name="finish",
    )(*parts, dual_rim)
    return (dict_spectra, dictionary)


def solution(mesh):
    placed = (
        P(("grp", "filt"), "band", None),
        P("grp", "band", None),
        P(("grp", "band"), None, None, "filt", None),
        P(("grp", "filt"), None),
    )
    return jax.shard_map(
        body,
        mesh=mesh,
        in_specs=placed,
        out_specs=(P(("grp", "band"), None, None, "filt", None), P(("grp", "filt"), None)),
        check_vma=False,
    )
```

```python
import math

import jax
import jax.numpy as jnp
import numpy as np
from jax import lax
from jax.experimental import pallas as pl
from jax.experimental.pallas import tpu as pltpu
from jax.sharding import PartitionSpec as P

K = 16
LANES = 128
HALF = 64
GROUP = 4
CHUNKS = 8

penalty = 1.0

bf16 = jnp.bfloat16
f32 = jnp.float32


def column_table(length, bands):
    ramp = np.arange(length)
    angles = (ramp[:, None] * ramp[None, :] % length) * (2.0 * math.pi / length)
    factor = 1.0 / math.sqrt(length)
    table = np.stack([np.cos(angles) * factor, -np.sin(angles) * factor], axis=1)
    table = table.reshape(length, 2, bands, length // bands).transpose(2, 0, 1, 3)
    return table.reshape(bands, length, 2 * length // bands).astype(np.float32).astype(bf16)


def row_table(height, band_rows):
    ramp = np.arange(height)
    angles = (ramp[:, None] * ramp[None, :] % height) * (2.0 * math.pi / height)
    factor = 1.0 / math.sqrt(height)
    cos, sin = np.cos(angles) * factor, np.sin(angles) * factor
    both = np.stack(
        [np.concatenate([cos, -sin], axis=1), np.concatenate([sin, cos], axis=1)]
    )
    both = both.reshape(2, height // band_rows, band_rows, 2 * height)
    table = np.zeros((2, height // band_rows, 2, band_rows, 2, 2 * height))
    table[:, :, 0, :, 0] = both
    table[:, :, 1, :, 1] = both
    return table.reshape(4 * height, 4 * height).astype(np.float32).astype(bf16)


def inverse_table(height, columns, width, group):
    reach = np.arange(width)
    rows = (np.arange(height)[:, None] * reach[None, :] % height) * (2.0 * math.pi / height)
    cols = (np.arange(group)[:, None] * reach[None, :] % columns) * (2.0 * math.pi / columns)
    turn = rows[None, :, :, None] + cols[:, None, None, :]
    factor = 1.0 / math.sqrt(height * columns)
    cos, sin = np.cos(turn) * factor, np.sin(turn) * factor
    table = np.stack([np.stack([cos, -sin], axis=1), np.stack([-sin, -cos], axis=1)], axis=3)
    return table.reshape(group * 2 * height, 2 * width * width).astype(np.float32).astype(bf16)


def turn_table(columns, width, group):
    reach = np.arange(width)
    first = np.arange(0, columns, group)
    turn = (first[:, None] * reach[None, :] % columns) * (2.0 * math.pi / columns)
    turn = np.tile(turn, (1, width))
    return np.concatenate([np.cos(turn), np.sin(turn)], axis=1).astype(np.float32)


def low_lanes(shape):
    return lax.broadcasted_iota(jnp.int32, shape, len(shape) - 1) < HALF


def columns_kernel(
    maps_ref, image_ref, table_ref, out_ref, maps_in, image_in, table_in, maps_sem, image_sem, table_sem
):
    bands = out_ref.shape[0]
    rows = maps_ref.shape[0]
    maps_copy = pltpu.make_async_copy(maps_ref, maps_in, maps_sem)
    image_copy = pltpu.make_async_copy(image_ref, image_in, image_sem)
    table_copies = [
        pltpu.make_async_copy(table_ref.at[b], table_in.at[b], table_sem.at[b]) for b in range(bands)
    ]
    maps_copy.start()
    image_copy.start()
    for copy in table_copies:
        copy.start()
    maps_copy.wait()
    image_copy.wait()
    for b in range(bands):
        table_copies[b].wait()
        table = table_in[b]
        out_ref[b, :rows] = jnp.dot(maps_in[...], table, preferred_element_type=f32).astype(bf16)
        out_ref[b, rows:] = jnp.dot(image_in[...], table, preferred_element_type=f32).astype(bf16)


def prepare_kernel(target_ref, packed_ref):
    freqs, _, channels, filters, height = target_ref.shape

    def step(q, carry):
        for c in range(channels):
            packed_ref[q, c] = jnp.concatenate(
                [target_ref[q, 0, c].astype(f32), target_ref[q, 1, c].astype(f32)], axis=-1
            )
        return carry

    lax.fori_loop(0, freqs, step, 0, unroll=2)


def rows_kernel(got_ref, table_ref, packed_ref, x_ref, image_ref, own_ref, send_ref, one_ref, two_ref):
    freqs, channels, filters, _ = packed_ref.shape
    sources, rows, _ = got_ref.shape
    band_rows = rows // (filters + channels)
    pair = 2 * band_rows
    table = table_ref[...]

    def transform(start):
        block = got_ref[:, start : start + pair, :].reshape(sources * pair, LANES)
        turned = block.T
        left = jnp.concatenate([turned[:freqs], turned[freqs:]], axis=1)
        return jnp.dot(left, table, preferred_element_type=f32)

    for j in range(filters // 2):
        both = transform(j * pair)
        x_ref[pl.ds(2 * j, freqs, stride=filters), :] = both[:, :LANES]
        x_ref[pl.ds(2 * j + 1, freqs, stride=filters), :] = both[:, LANES:]
    for c in range(channels):
        first = min(c, channels - 2)
        both = transform((filters + first) * band_rows)
        part = (c - first) * LANES
        image_ref[c * freqs : (c + 1) * freqs, :] = both[:, part : part + LANES]

    group = 8

    def step(i, carry):
        q0 = pl.multiple_of(i * group, group)
        x = x_ref[pl.ds(pl.multiple_of(q0 * filters, group * filters), group * filters), :]
        y = pltpu.roll(x, HALF, 1)
        x = x.reshape(group, filters, LANES)
        y = y.reshape(group, filters, LANES)
        one_ref[pl.ds(channels * freqs + q0, group), :] = jnp.sum(x * x, axis=1)
        for c in range(channels):
            v = packed_ref[pl.ds(q0, group), c]
            one_ref[pl.ds(c * freqs + q0, group), :] = jnp.sum(x * v, axis=1)
            two_ref[pl.ds(c * freqs + q0, group), :] = jnp.sum(y * v, axis=1)
        return carry

    lax.fori_loop(0, freqs // group, step, 0)
    top = channels * freqs
    one = one_ref[:top]
    two = two_ref[...]
    low = low_lanes(one.shape)
    cross = jnp.where(low, one - pltpu.roll(one, HALF, 1), two + pltpu.roll(two, HALF, 1))
    energy = one_ref[top:]
    energy = energy + pltpu.roll(energy, HALF, 1)
    own_ref[:top] = cross
    own_ref[top:] = energy
    send_ref[:top] = cross.astype(bf16)
    send_ref[top:] = energy.astype(bf16)


def solve_kernel(
    x_ref,
    packed_ref,
    image_ref,
    own_ref,
    peer_ref,
    inverse_ref,
    turn_ref,
    out_ref,
    rim_ref,
    re_ref,
    im_ref,
    held_ref,
    sems,
):
    freqs, channels, filters, _ = packed_ref.shape
    group = inverse_ref.shape[0] // LANES
    area = rim_ref.shape[1]
    lines = channels * filters
    top = channels * freqs
    total = own_ref[...] + peer_ref[...].astype(f32)
    denom = penalty + total[top:]
    low = low_lanes(denom.shape)
    for c in range(channels):
        span = slice(c * freqs, (c + 1) * freqs)
        coef = (image_ref[span] - total[span]) / denom
        turned = pltpu.roll(coef, HALF, 1)
        re_ref[span] = jnp.where(low, coef, -turned)
        im_ref[span] = jnp.where(low, turned, coef)

    chunk = freqs // CHUNKS

    def written(i):
        span = pl.ds(i * chunk, chunk)
        return pltpu.make_async_copy(held_ref.at[span], out_ref.at[span], sems.at[i])

    def step(i, acc):
        blocks = []
        for j in range(chunk // group):
            sides = []
            for k in range(group):
                q = i * chunk + j * group + k
                x = x_ref[pl.ds(pl.multiple_of(q * filters, filters), filters), :]
                y = pltpu.roll(x, HALF, 1)
                parts = []
                for c in range(channels):
                    d = (
                        packed_ref[q, c]
                        + x * re_ref[pl.ds(c * freqs + q, 1), :]
                        + y * im_ref[pl.ds(c * freqs + q, 1), :]
                    )
                    d = d.astype(bf16)
                    held_ref[q, 0, c] = d[:, :HALF]
                    held_ref[q, 1, c] = d[:, HALF:]
                    parts.append(d)
                sides.append(jnp.concatenate(parts, axis=0))
            blocks.append(jnp.concatenate(sides, axis=1))
        written(i).start()
        left = jnp.concatenate(blocks, axis=0)
        both = jnp.dot(left, inverse_ref[...], preferred_element_type=f32)
        for j in range(chunk // group):
            line = i * (chunk // group) + j
            part = both[j * lines : (j + 1) * lines] * turn_ref[pl.ds(line, 1), :]
            acc = acc + (part[:, :area] + part[:, area:])
        return acc

    acc = lax.fori_loop(0, CHUNKS, step, jnp.zeros(rim_ref.shape, f32))
    rim_ref[...] = acc.astype(bf16)
    for i in range(CHUNKS):
        written(i).wait()


def finish_kernel(*refs):
    part_refs, dual_ref, out_ref = refs[:-2], refs[-2], refs[-1]
    filters = dual_ref.shape[0]
    sums = [r[...].astype(f32) for r in part_refs]
    while len(sums) > 1:
        sums = [sums[i] + sums[i + 1] for i in range(0, len(sums), 2)]
    area = sums[0].shape[1]
    channels = sums[0].shape[0] // filters
    joined = [
        sums[0][c * filters : (c + 1) * filters] + dual_ref[:, c * area : (c + 1) * area]
        for c in range(channels)
    ]
    squares = sum(jnp.sum(w * w, axis=1, keepdims=True) for w in joined)
    spread = jnp.sqrt(squares / (channels * area))
    scale = jnp.maximum(spread, 1.0)
    for c in range(channels):
        out_ref[:, c * area : (c + 1) * area] = joined[c] / scale


def params(mib):
    return pltpu.CompilerParams(vmem_limit_bytes=mib * 1024 * 1024)


def far(array):
    return pltpu.with_memory_space_constraint(array, pltpu.HBM)


def add_kernel(a_ref, b_ref, out_ref):
    out_ref[...] = (a_ref[...].astype(f32) + b_ref[...].astype(f32)).astype(bf16)


def plain(coeff_maps, image, target, dual_rim):
    filters, band_rows, width_cols = coeff_maps.shape
    channels = image.shape[0]
    bands = lax.axis_size("band")
    height = band_rows * bands
    freqs = width_cols // bands
    table = jnp.asarray(column_table(width_cols, bands))
    stacked = jnp.concatenate([coeff_maps, image], axis=0)
    send = jnp.einsum("mrn,bnk->brmk", stacked, table, preferred_element_type=f32)
    got = lax.all_to_all(send.astype(bf16), "band", split_axis=0, concat_axis=0)
    got = got.reshape(height, filters + channels, 2, freqs)
    ramp = jnp.arange(height, dtype=jnp.int32)
    angles = (ramp[:, None] * ramp[None, :] % height).astype(f32) * (2.0 * math.pi / height)
    factor = 1.0 / math.sqrt(height)
    lookup = jnp.stack([jnp.cos(angles) * factor, jnp.sin(angles) * factor]).astype(bf16)
    both = jnp.einsum("hmpq,tgh->ptqmg", got, lookup, preferred_element_type=f32)
    re = both[0, 0] + both[1, 1]
    im = both[1, 0] - both[0, 1]
    x_re, s_re = re[:, :filters], re[:, filters:]
    x_im, s_im = im[:, :filters], im[:, filters:]
    v_re = target[:, 0].astype(f32)
    v_im = target[:, 1].astype(f32)
    energy = jnp.sum(x_re * x_re + x_im * x_im, axis=1)
    cross_re = jnp.sum(x_re[:, None] * v_re - x_im[:, None] * v_im, axis=2)
    cross_im = jnp.sum(x_re[:, None] * v_im + x_im[:, None] * v_re, axis=2)
    sums = jnp.concatenate([cross_re, cross_im, energy[:, None]], axis=1)
    sums = lax.psum(sums.astype(bf16), "filt").astype(f32)
    denom = penalty + sums[:, 2 * channels :]
    coef_re = ((s_re - sums[:, :channels]) / denom)[:, :, None]
    coef_im = ((s_im - sums[:, channels : 2 * channels]) / denom)[:, :, None]
    d_re = v_re + x_re[:, None] * coef_re + x_im[:, None] * coef_im
    d_im = v_im + x_re[:, None] * coef_im - x_im[:, None] * coef_re
    reach = jnp.arange(K, dtype=jnp.int32)
    rows = (ramp[:, None] * reach[None, :] % height).astype(f32) * (2.0 * math.pi / height)
    cols = lax.axis_index("band") * freqs + jnp.arange(freqs, dtype=jnp.int32)
    cols = (cols[:, None] * reach[None, :] % width_cols).astype(f32) * (2.0 * math.pi / width_cols)
    turn = rows[None, :, :, None] + cols[:, None, None, :]
    factor = 1.0 / math.sqrt(height * width_cols)
    exact = lax.Precision.HIGHEST
    spatial = jnp.einsum("qcmg,qgyx->mcyx", d_re, jnp.cos(turn) * factor, precision=exact)
    spatial -= jnp.einsum("qcmg,qgyx->mcyx", d_im, jnp.sin(turn) * factor, precision=exact)
    spatial = lax.psum(spatial.reshape(dual_rim.shape), "band")
    joined = spatial + dual_rim
    spread = jnp.sqrt(jnp.mean(joined * joined, axis=1, keepdims=True))
    dict_spectra = jnp.stack([d_re, d_im], axis=1).astype(bf16)
    return (dict_spectra, joined / jnp.maximum(spread, 1.0))


def body(coeff_maps, image, target, dual_rim):
    filters, band_rows, width_cols = coeff_maps.shape
    channels = image.shape[0]
    bands = lax.axis_size("band")
    height = band_rows * bands
    freqs = width_cols // bands
    rows = (filters + channels) * band_rows
    if (2 * freqs, 2 * height, 16 % band_rows, filters % 2, bands & (bands - 1)) != (LANES, LANES, 0, 0, 0):
        return plain(coeff_maps, image, target, dual_rim)

    send = pl.pallas_call(
        columns_kernel,
        out_shape=jax.ShapeDtypeStruct((bands, rows, LANES), bf16),
        in_specs=[pl.BlockSpec(memory_space=pltpu.HBM)] * 3,
        scratch_shapes=[
            pltpu.VMEM((filters * band_rows, width_cols), bf16),
            pltpu.VMEM((channels * band_rows, width_cols), bf16),
            pltpu.VMEM((bands, width_cols, LANES), bf16),
            pltpu.SemaphoreType.DMA,
            pltpu.SemaphoreType.DMA,
            pltpu.SemaphoreType.DMA((bands,)),
        ],
        compiler_params=params(8),
        name="columns",
    )(
        far(coeff_maps.reshape(filters * band_rows, width_cols)),
        far(image.reshape(channels * band_rows, width_cols)),
        far(jnp.asarray(column_table(width_cols, bands))),
    )
    got = lax.all_to_all(send, "band", split_axis=0, concat_axis=0)

    groups = freqs // GROUP
    turns = jnp.asarray(turn_table(width_cols, K, GROUP))
    turns = lax.dynamic_slice_in_dim(turns, lax.axis_index("band") * groups, groups, axis=0)
    packed = pl.pallas_call(
        prepare_kernel,
        out_shape=jax.ShapeDtypeStruct((freqs, channels, filters, LANES), f32),
        compiler_params=params(12),
        name="prepare",
    )(target)

    lines = (channels + 1) * freqs
    x, lit, own, sums = pl.pallas_call(
        rows_kernel,
        out_shape=(
            jax.ShapeDtypeStruct((freqs * filters, LANES), f32),
            jax.ShapeDtypeStruct((channels * freqs, LANES), f32),
            jax.ShapeDtypeStruct((lines, LANES), f32),
            jax.ShapeDtypeStruct((lines, LANES), bf16),
        ),
        scratch_shapes=[
            pltpu.VMEM((lines, LANES), f32),
            pltpu.VMEM((channels * freqs, LANES), f32),
        ],
        compiler_params=params(8),
        name="rows",
    )(got, jnp.asarray(row_table(height, band_rows)), packed)

    peer = lax.ppermute(sums, "filt", [(0, 1), (1, 0)])

    dict_spectra, rim = pl.pallas_call(
        solve_kernel,
        out_shape=(
            jax.ShapeDtypeStruct(target.shape, bf16),
            jax.ShapeDtypeStruct((channels * filters, K * K), bf16),
        ),
        out_specs=(pl.BlockSpec(memory_space=pltpu.HBM), pl.BlockSpec(memory_space=pltpu.VMEM)),
        scratch_shapes=[
            pltpu.VMEM((channels * freqs, LANES), f32),
            pltpu.VMEM((channels * freqs, LANES), f32),
            pltpu.VMEM(target.shape, bf16),
            pltpu.SemaphoreType.DMA((CHUNKS,)),
        ],
        compiler_params=params(16),
        name="solve",
    )(x, packed, lit, own, peer, jnp.asarray(inverse_table(height, width_cols, K, GROUP)), turns)

    near = lax.ppermute(rim, "band", [(i, i ^ 1) for i in range(bands)])
    pair = pl.pallas_call(
        add_kernel,
        out_shape=jax.ShapeDtypeStruct(rim.shape, bf16),
        compiler_params=params(4),
        name="add",
    )(rim, near)
    parts = [pair] + [
        lax.ppermute(pair, "band", [(i, i ^ k) for i in range(bands)]) for k in range(2, bands, 2)
    ]
    dictionary = pl.pallas_call(
        finish_kernel,
        out_shape=jax.ShapeDtypeStruct(dual_rim.shape, f32),
        compiler_params=params(4),
        name="finish",
    )(*parts, dual_rim)
    return (dict_spectra, dictionary)


def solution(mesh):
    placed = (
        P(("grp", "filt"), "band", None),
        P("grp", "band", None),
        P(("grp", "band"), None, None, "filt", None),
        P(("grp", "filt"), None),
    )
    return jax.shard_map(
        body,
        mesh=mesh,
        in_specs=placed,
        out_specs=(P(("grp", "band"), None, None, "filt", None), P(("grp", "filt"), None)),
        check_vma=False,
    )
```

```python
import math

import jax
import jax.numpy as jnp
import numpy as np
from jax import lax
from jax.experimental import pallas as pl
from jax.experimental.pallas import tpu as pltpu
from jax.sharding import PartitionSpec as P

K = 16
LANES = 128
HALF = 64
GROUP = 4
CHUNKS = 8

penalty = 1.0

bf16 = jnp.bfloat16
f32 = jnp.float32


def column_table(length, bands):
    ramp = np.arange(length)
    angles = (ramp[:, None] * ramp[None, :] % length) * (2.0 * math.pi / length)
    factor = 1.0 / math.sqrt(length)
    table = np.stack([np.cos(angles) * factor, -np.sin(angles) * factor], axis=1)
    table = table.reshape(length, 2, bands, length // bands).transpose(2, 0, 1, 3)
    return table.reshape(bands, length, 2 * length // bands).astype(np.float32).astype(bf16)


def row_table(height, band_rows):
    ramp = np.arange(height)
    angles = (ramp[:, None] * ramp[None, :] % height) * (2.0 * math.pi / height)
    factor = 1.0 / math.sqrt(height)
    cos, sin = np.cos(angles) * factor, np.sin(angles) * factor
    both = np.stack(
        [np.concatenate([cos, -sin], axis=1), np.concatenate([sin, cos], axis=1)]
    )
    both = both.reshape(2, height // band_rows, band_rows, 2 * height)
    table = np.zeros((2, height // band_rows, 2, band_rows, 2, 2 * height))
    table[:, :, 0, :, 0] = both
    table[:, :, 1, :, 1] = both
    table = table.reshape(2, height // band_rows, 2 * band_rows, 4 * height)
    return table.astype(np.float32).astype(bf16)


def inverse_table(height, columns, width, group):
    reach = np.arange(width)
    rows = (np.arange(height)[:, None] * reach[None, :] % height) * (2.0 * math.pi / height)
    cols = (np.arange(group)[:, None] * reach[None, :] % columns) * (2.0 * math.pi / columns)
    turn = rows[None, :, :, None] + cols[:, None, None, :]
    factor = 1.0 / math.sqrt(height * columns)
    cos, sin = np.cos(turn) * factor, np.sin(turn) * factor
    table = np.stack([np.stack([cos, -sin], axis=1), np.stack([-sin, -cos], axis=1)], axis=3)
    return table.reshape(group * 2 * height, 2 * width * width).astype(np.float32).astype(bf16)


def turn_table(columns, width, group):
    reach = np.arange(width)
    first = np.arange(0, columns, group)
    turn = (first[:, None] * reach[None, :] % columns) * (2.0 * math.pi / columns)
    turn = np.tile(turn, (1, width))
    return np.concatenate([np.cos(turn), np.sin(turn)], axis=1).astype(np.float32)


def far_first(bands):
    if bands == 8:
        return [4, 2, 6, 5, 3, 7, 1, 0]
    return list(range(bands - 1, -1, -1))


def low_lanes(shape):
    return lax.broadcasted_iota(jnp.int32, shape, len(shape) - 1) < HALF


def columns_kernel(maps_ref, image_ref, table_ref, *refs):
    out_refs = refs[:-4]
    lines_in, table_in, line_sem, table_sem = refs[-4:]
    bands = len(out_refs)
    rows = maps_ref.shape[0]
    mine = lax.axis_index("band")
    maps_copy = pltpu.make_async_copy(maps_ref, lines_in.at[:rows], line_sem.at[0])
    image_copy = pltpu.make_async_copy(image_ref, lines_in.at[rows:], line_sem.at[1])
    table_copies = [
        pltpu.make_async_copy(
            table_ref.at[mine ^ k],
            table_in.at[i // 2, :, i % 2 * LANES : (i % 2 + 1) * LANES],
            table_sem.at[i],
        )
        for i, k in enumerate(far_first(bands))
    ]
    maps_copy.start()
    image_copy.start()
    for copy in table_copies:
        copy.start()
    maps_copy.wait()
    image_copy.wait()
    for i in range(0, bands, 2):
        table_copies[i].wait()
        table_copies[i + 1].wait()
        both = jnp.dot(lines_in[...], table_in[i // 2], preferred_element_type=f32).astype(bf16)
        out_refs[i][...] = both[:, :LANES]
        out_refs[i + 1][...] = both[:, LANES:]


def prepare_kernel(target_ref, packed_ref, target_in, sems):
    freqs, _, channels, filters, height = target_ref.shape
    chunk = freqs // CHUNKS

    def fetched(i):
        span = pl.ds(i * chunk, chunk)
        return pltpu.make_async_copy(target_ref.at[span], target_in.at[span], sems.at[i])

    for i in range(CHUNKS):
        fetched(i).start()

    def step(i, carry):
        fetched(i).wait()
        for j in range(chunk):
            q = i * chunk + j
            for c in range(channels):
                packed_ref[q, c] = jnp.concatenate(
                    [target_in[q, 0, c].astype(f32), target_in[q, 1, c].astype(f32)], axis=-1
                )
        return carry

    lax.fori_loop(0, CHUNKS, step, 0)


def rows_kernel(*refs):
    got_refs = refs[:-8]
    table_ref, packed_ref, x_ref, image_ref, own_ref, send_ref, one_ref, two_ref = refs[-8:]
    freqs, channels, filters, _ = packed_ref.shape
    sources = len(got_refs)
    band_rows = got_refs[0].shape[0] // (filters + channels)
    pair = 2 * band_rows
    mine = lax.axis_index("band")
    table = jnp.concatenate([table_ref[p, mine ^ k] for p in range(2) for k in far_first(sources)], axis=0)

    def transform(start):
        block = jnp.concatenate([ref[start : start + pair, :] for ref in got_refs], axis=0)
        turned = block.T
        left = jnp.concatenate([turned[:freqs], turned[freqs:]], axis=1)
        return jnp.dot(left, table, preferred_element_type=f32)

    for j in range(filters // 2):
        both = transform(j * pair)
        x_ref[pl.ds(2 * j, freqs, stride=filters), :] = both[:, :LANES]
        x_ref[pl.ds(2 * j + 1, freqs, stride=filters), :] = both[:, LANES:]
    for c in range(channels):
        first = min(c, channels - 2)
        both = transform((filters + first) * band_rows)
        part = (c - first) * LANES
        image_ref[c * freqs : (c + 1) * freqs, :] = both[:, part : part + LANES]

    group = 8

    def step(i, carry):
        q0 = pl.multiple_of(i * group, group)
        x = x_ref[pl.ds(pl.multiple_of(q0 * filters, group * filters), group * filters), :]
        y = pltpu.roll(x, HALF, 1)
        x = x.reshape(group, filters, LANES)
        y = y.reshape(group, filters, LANES)
        one_ref[pl.ds(channels * freqs + q0, group), :] = jnp.sum(x * x, axis=1)
        for c in range(channels):
            v = packed_ref[pl.ds(q0, group), c]
            one_ref[pl.ds(c * freqs + q0, group), :] = jnp.sum(x * v, axis=1)
            two_ref[pl.ds(c * freqs + q0, group), :] = jnp.sum(y * v, axis=1)
        return carry

    lax.fori_loop(0, freqs // group, step, 0)
    top = channels * freqs
    one = one_ref[:top]
    two = two_ref[...]
    low = low_lanes(one.shape)
    cross = jnp.where(low, one - pltpu.roll(one, HALF, 1), two + pltpu.roll(two, HALF, 1))
    energy = one_ref[top:]
    energy = energy + pltpu.roll(energy, HALF, 1)
    own_ref[:top] = cross
    own_ref[top:] = energy
    send_ref[:top] = cross.astype(bf16)
    send_ref[top:] = energy.astype(bf16)


def solve_kernel(
    x_ref,
    packed_ref,
    image_ref,
    own_ref,
    peer_ref,
    inverse_ref,
    turn_ref,
    out_ref,
    rim_ref,
    re_ref,
    im_ref,
    held_ref,
    sems,
):
    freqs, channels, filters, _ = packed_ref.shape
    group = inverse_ref.shape[0] // LANES
    area = rim_ref.shape[1]
    lines = channels * filters
    top = channels * freqs
    total = own_ref[...] + peer_ref[...].astype(f32)
    denom = penalty + total[top:]
    low = low_lanes(denom.shape)
    for c in range(channels):
        span = slice(c * freqs, (c + 1) * freqs)
        coef = (image_ref[span] - total[span]) / denom
        turned = pltpu.roll(coef, HALF, 1)
        re_ref[span] = jnp.where(low, coef, -turned)
        im_ref[span] = jnp.where(low, turned, coef)

    chunk = freqs // CHUNKS
    mine = lax.axis_index("band")

    def written(i):
        span = pl.ds(i * chunk, chunk)
        return pltpu.make_async_copy(held_ref.at[span], out_ref.at[span], sems.at[i])

    def step(i, acc):
        blocks = []
        for j in range(chunk // group):
            sides = []
            for k in range(group):
                q = i * chunk + j * group + k
                x = x_ref[pl.ds(pl.multiple_of(q * filters, filters), filters), :]
                y = pltpu.roll(x, HALF, 1)
                parts = []
                for c in range(channels):
                    d = (
                        packed_ref[q, c]
                        + x * re_ref[pl.ds(c * freqs + q, 1), :]
                        + y * im_ref[pl.ds(c * freqs + q, 1), :]
                    )
                    d = d.astype(bf16)
                    held_ref[q, 0, c] = d[:, :HALF]
                    held_ref[q, 1, c] = d[:, HALF:]
                    parts.append(d)
                sides.append(jnp.concatenate(parts, axis=0))
            blocks.append(jnp.concatenate(sides, axis=1))
        written(i).start()
        left = jnp.concatenate(blocks, axis=0)
        both = jnp.dot(left, inverse_ref[...], preferred_element_type=f32)
        for j in range(chunk // group):
            line = i * (chunk // group) + j
            part = both[j * lines : (j + 1) * lines] * turn_ref[mine, pl.ds(line, 1), :]
            acc = acc + (part[:, :area] + part[:, area:])
        return acc

    acc = lax.fori_loop(0, CHUNKS, step, jnp.zeros(rim_ref.shape, f32))
    rim_ref[...] = acc.astype(bf16)
    for i in range(CHUNKS):
        written(i).wait()


def finish_kernel(*refs):
    part_refs, dual_ref, out_ref = refs[:-2], refs[-2], refs[-1]
    filters = dual_ref.shape[0]
    sums = [r[...].astype(f32) for r in part_refs]
    while len(sums) > 1:
        sums = [sums[i] + sums[i + 1] for i in range(0, len(sums), 2)]
    area = sums[0].shape[1]
    channels = sums[0].shape[0] // filters
    joined = [
        sums[0][c * filters : (c + 1) * filters] + dual_ref[:, c * area : (c + 1) * area]
        for c in range(channels)
    ]
    squares = sum(jnp.sum(w * w, axis=1, keepdims=True) for w in joined)
    spread = jnp.sqrt(squares / (channels * area))
    scale = jnp.maximum(spread, 1.0)
    for c in range(channels):
        out_ref[:, c * area : (c + 1) * area] = joined[c] / scale


def params(mib):
    return pltpu.CompilerParams(vmem_limit_bytes=mib * 1024 * 1024)


def far(array):
    return pltpu.with_memory_space_constraint(array, pltpu.HBM)


def add_kernel(a_ref, b_ref, out_ref):
    out_ref[...] = (a_ref[...].astype(f32) + b_ref[...].astype(f32)).astype(bf16)


def plain(coeff_maps, image, target, dual_rim):
    filters, band_rows, width_cols = coeff_maps.shape
    channels = image.shape[0]
    bands = lax.axis_size("band")
    height = band_rows * bands
    freqs = width_cols // bands
    table = jnp.asarray(column_table(width_cols, bands))
    stacked = jnp.concatenate([coeff_maps, image], axis=0)
    send = jnp.einsum("mrn,bnk->brmk", stacked, table, preferred_element_type=f32)
    got = lax.all_to_all(send.astype(bf16), "band", split_axis=0, concat_axis=0)
    got = got.reshape(height, filters + channels, 2, freqs)
    ramp = jnp.arange(height, dtype=jnp.int32)
    angles = (ramp[:, None] * ramp[None, :] % height).astype(f32) * (2.0 * math.pi / height)
    factor = 1.0 / math.sqrt(height)
    lookup = jnp.stack([jnp.cos(angles) * factor, jnp.sin(angles) * factor]).astype(bf16)
    both = jnp.einsum("hmpq,tgh->ptqmg", got, lookup, preferred_element_type=f32)
    re = both[0, 0] + both[1, 1]
    im = both[1, 0] - both[0, 1]
    x_re, s_re = re[:, :filters], re[:, filters:]
    x_im, s_im = im[:, :filters], im[:, filters:]
    v_re = target[:, 0].astype(f32)
    v_im = target[:, 1].astype(f32)
    energy = jnp.sum(x_re * x_re + x_im * x_im, axis=1)
    cross_re = jnp.sum(x_re[:, None] * v_re - x_im[:, None] * v_im, axis=2)
    cross_im = jnp.sum(x_re[:, None] * v_im + x_im[:, None] * v_re, axis=2)
    sums = jnp.concatenate([cross_re, cross_im, energy[:, None]], axis=1)
    sums = lax.psum(sums.astype(bf16), "filt").astype(f32)
    denom = penalty + sums[:, 2 * channels :]
    coef_re = ((s_re - sums[:, :channels]) / denom)[:, :, None]
    coef_im = ((s_im - sums[:, channels : 2 * channels]) / denom)[:, :, None]
    d_re = v_re + x_re[:, None] * coef_re + x_im[:, None] * coef_im
    d_im = v_im + x_re[:, None] * coef_im - x_im[:, None] * coef_re
    reach = jnp.arange(K, dtype=jnp.int32)
    rows = (ramp[:, None] * reach[None, :] % height).astype(f32) * (2.0 * math.pi / height)
    cols = lax.axis_index("band") * freqs + jnp.arange(freqs, dtype=jnp.int32)
    cols = (cols[:, None] * reach[None, :] % width_cols).astype(f32) * (2.0 * math.pi / width_cols)
    turn = rows[None, :, :, None] + cols[:, None, None, :]
    factor = 1.0 / math.sqrt(height * width_cols)
    exact = lax.Precision.HIGHEST
    spatial = jnp.einsum("qcmg,qgyx->mcyx", d_re, jnp.cos(turn) * factor, precision=exact)
    spatial -= jnp.einsum("qcmg,qgyx->mcyx", d_im, jnp.sin(turn) * factor, precision=exact)
    spatial = lax.psum(spatial.reshape(dual_rim.shape), "band")
    joined = spatial + dual_rim
    spread = jnp.sqrt(jnp.mean(joined * joined, axis=1, keepdims=True))
    dict_spectra = jnp.stack([d_re, d_im], axis=1).astype(bf16)
    return (dict_spectra, joined / jnp.maximum(spread, 1.0))


def body(coeff_maps, image, target, dual_rim):
    filters, band_rows, width_cols = coeff_maps.shape
    channels = image.shape[0]
    bands = lax.axis_size("band")
    height = band_rows * bands
    freqs = width_cols // bands
    rows = (filters + channels) * band_rows
    if (2 * freqs, 2 * height, 16 % band_rows, filters % 2, bands & (bands - 1)) != (LANES, LANES, 0, 0, 0):
        return plain(coeff_maps, image, target, dual_rim)

    def swap(array, k):
        return lax.ppermute(array, "band", [(i, i ^ k) for i in range(bands)])

    chunks = pl.pallas_call(
        columns_kernel,
        out_shape=(jax.ShapeDtypeStruct((rows, LANES), bf16),) * bands,
        in_specs=[pl.BlockSpec(memory_space=pltpu.HBM)] * 3,
        scratch_shapes=[
            pltpu.VMEM((rows, width_cols), bf16),
            pltpu.VMEM((bands // 2, width_cols, 2 * LANES), bf16),
            pltpu.SemaphoreType.DMA((2,)),
            pltpu.SemaphoreType.DMA((bands,)),
        ],
        compiler_params=params(8),
        name="columns",
    )(
        far(coeff_maps.reshape(filters * band_rows, width_cols)),
        far(image.reshape(channels * band_rows, width_cols)),
        far(jnp.asarray(column_table(width_cols, bands))),
    )
    got = [swap(chunk, k) if k else chunk for k, chunk in zip(far_first(bands), chunks)]

    turns = turn_table(width_cols, K, GROUP).reshape(bands, freqs // GROUP, 2 * K * K)
    packed = pl.pallas_call(
        prepare_kernel,
        out_shape=jax.ShapeDtypeStruct((freqs, channels, filters, LANES), f32),
        in_specs=[pl.BlockSpec(memory_space=pltpu.HBM)],
        scratch_shapes=[pltpu.VMEM(target.shape, bf16), pltpu.SemaphoreType.DMA((CHUNKS,))],
        compiler_params=params(12),
        name="prepare",
    )(far(target))

    lines = (channels + 1) * freqs
    x, lit, own, sums = pl.pallas_call(
        rows_kernel,
        out_shape=(
            jax.ShapeDtypeStruct((freqs * filters, LANES), f32),
            jax.ShapeDtypeStruct((channels * freqs, LANES), f32),
            jax.ShapeDtypeStruct((lines, LANES), f32),
            jax.ShapeDtypeStruct((lines, LANES), bf16),
        ),
        scratch_shapes=[
            pltpu.VMEM((lines, LANES), f32),
            pltpu.VMEM((channels * freqs, LANES), f32),
        ],
        compiler_params=params(8),
        name="rows",
    )(*got, jnp.asarray(row_table(height, band_rows)), packed)

    peer = lax.ppermute(sums, "filt", [(0, 1), (1, 0)])

    dict_spectra, rim = pl.pallas_call(
        solve_kernel,
        out_shape=(
            jax.ShapeDtypeStruct(target.shape, bf16),
            jax.ShapeDtypeStruct((channels * filters, K * K), bf16),
        ),
        out_specs=(pl.BlockSpec(memory_space=pltpu.HBM), pl.BlockSpec(memory_space=pltpu.VMEM)),
        scratch_shapes=[
            pltpu.VMEM((channels * freqs, LANES), f32),
            pltpu.VMEM((channels * freqs, LANES), f32),
            pltpu.VMEM(target.shape, bf16),
            pltpu.SemaphoreType.DMA((CHUNKS,)),
        ],
        compiler_params=params(16),
        name="solve",
    )(x, packed, lit, own, peer, jnp.asarray(inverse_table(height, width_cols, K, GROUP)), jnp.asarray(turns))

    near = swap(rim, 1)
    pair = pl.pallas_call(
        add_kernel,
        out_shape=jax.ShapeDtypeStruct(rim.shape, bf16),
        compiler_params=params(4),
        name="add",
    )(rim, near)
    parts = [pair] + [swap(pair, k) for k in range(2, bands, 2)]
    dictionary = pl.pallas_call(
        finish_kernel,
        out_shape=jax.ShapeDtypeStruct(dual_rim.shape, f32),
        compiler_params=params(4),
        name="finish",
    )(*parts, dual_rim)
    return (dict_spectra, dictionary)


def solution(mesh):
    placed = (
        P(("grp", "filt"), "band", None),
        P("grp", "band", None),
        P(("grp", "band"), None, None, "filt", None),
        P(("grp", "filt"), None),
    )
    return jax.shard_map(
        body,
        mesh=mesh,
        in_specs=placed,
        out_specs=(P(("grp", "band"), None, None, "filt", None), P(("grp", "filt"), None)),
        check_vma=False,
    )
```

```python
import math

import jax
import jax.numpy as jnp
import numpy as np
from jax import lax
from jax.experimental import pallas as pl
from jax.experimental.pallas import tpu as pltpu
from jax.sharding import PartitionSpec as P

K = 16
LANES = 128
HALF = 64
GROUP = 4
CHUNKS = 8

penalty = 1.0

bf16 = jnp.bfloat16
f32 = jnp.float32


def column_table(length, bands):
    ramp = np.arange(length)
    angles = (ramp[:, None] * ramp[None, :] % length) * (2.0 * math.pi / length)
    factor = 1.0 / math.sqrt(length)
    table = np.stack([np.cos(angles) * factor, -np.sin(angles) * factor], axis=1)
    table = table.reshape(length, 2, bands, length // bands).transpose(2, 0, 1, 3)
    return table.reshape(bands, length, 2 * length // bands).astype(np.float32).astype(bf16)


def row_table(height, band_rows):
    ramp = np.arange(height)
    angles = (ramp[:, None] * ramp[None, :] % height) * (2.0 * math.pi / height)
    factor = 1.0 / math.sqrt(height)
    cos, sin = np.cos(angles) * factor, np.sin(angles) * factor
    both = np.stack(
        [np.concatenate([cos, -sin], axis=1), np.concatenate([sin, cos], axis=1)]
    )
    both = both.reshape(2, height // band_rows, band_rows, 2 * height)
    table = np.zeros((2, height // band_rows, 2, band_rows, 2, 2 * height))
    table[:, :, 0, :, 0] = both
    table[:, :, 1, :, 1] = both
    table = table.reshape(2, height // band_rows, 2 * band_rows, 4 * height)
    return table.astype(np.float32).astype(bf16)


def inverse_table(height, columns, width, group):
    reach = np.arange(width)
    rows = (np.arange(height)[:, None] * reach[None, :] % height) * (2.0 * math.pi / height)
    cols = (np.arange(group)[:, None] * reach[None, :] % columns) * (2.0 * math.pi / columns)
    turn = rows[None, :, :, None] + cols[:, None, None, :]
    factor = 1.0 / math.sqrt(height * columns)
    cos, sin = np.cos(turn) * factor, np.sin(turn) * factor
    table = np.stack([np.stack([cos, -sin], axis=1), np.stack([-sin, -cos], axis=1)], axis=3)
    return table.reshape(group * 2 * height, 2 * width * width).astype(np.float32).astype(bf16)


def turn_table(columns, width, group):
    reach = np.arange(width)
    first = np.arange(0, columns, group)
    turn = (first[:, None] * reach[None, :] % columns) * (2.0 * math.pi / columns)
    turn = np.tile(turn, (1, width))
    return np.concatenate([np.cos(turn), np.sin(turn)], axis=1).astype(np.float32)


def far_first(bands):
    if bands == 8:
        return [7, 1, 5, 2, 3, 4, 6, 0]
    return list(range(bands - 1, -1, -1))


def low_lanes(shape):
    return lax.broadcasted_iota(jnp.int32, shape, len(shape) - 1) < HALF


def columns_kernel(maps_ref, image_ref, table_ref, *refs):
    out_refs = refs[:-5]
    lines_in, both_in, table_in, line_sem, table_sem = refs[-5:]
    half = len(out_refs) // 2
    rows = maps_ref.shape[0]
    lines = lines_in.shape[0]
    mine = lax.axis_index("band")
    maps_copy = pltpu.make_async_copy(maps_ref, lines_in.at[:rows], line_sem.at[0])
    image_copy = pltpu.make_async_copy(image_ref, lines_in.at[rows:], line_sem.at[1])
    table_copies = [
        pltpu.make_async_copy(
            table_ref.at[(mine ^ k) % half],
            table_in.at[k // 2, :, k % 2 * LANES : (k % 2 + 1) * LANES],
            table_sem.at[k],
        )
        for k in range(half)
    ]
    maps_copy.start()
    image_copy.start()
    for copy in table_copies:
        copy.start()
    odd = lax.broadcasted_iota(jnp.int32, (1, lines_in.shape[1]), 1) % 2
    upper = (mine >= half).astype(jnp.int32)
    near_sign = (1 - 2 * odd * upper).astype(f32).astype(bf16)
    far_sign = (1 - 2 * odd * (1 - upper)).astype(f32).astype(bf16)
    maps_copy.wait()
    image_copy.wait()
    both_in[:lines] = lines_in[...] * near_sign
    both_in[lines:] = lines_in[...] * far_sign
    for k in range(0, half, 2):
        table_copies[k].wait()
        table_copies[k + 1].wait()
        both = jnp.dot(both_in[...], table_in[k // 2], preferred_element_type=f32).astype(bf16)
        out_refs[k][...] = both[:lines, :LANES]
        out_refs[k + 1][...] = both[:lines, LANES:]
        out_refs[half + k][...] = both[lines:, :LANES]
        out_refs[half + k + 1][...] = both[lines:, LANES:]


def prepare_kernel(target_ref, packed_ref, target_in, sems):
    freqs, _, channels, filters, height = target_ref.shape
    chunk = freqs // CHUNKS

    def fetched(i):
        span = pl.ds(i * chunk, chunk)
        return pltpu.make_async_copy(target_ref.at[span], target_in.at[span], sems.at[i])

    for i in range(CHUNKS):
        fetched(i).start()

    def step(i, carry):
        fetched(i).wait()
        for j in range(chunk):
            q = i * chunk + j
            for c in range(channels):
                packed_ref[q, c] = jnp.concatenate(
                    [target_in[q, 0, c].astype(f32), target_in[q, 1, c].astype(f32)], axis=-1
                )
        return carry

    lax.fori_loop(0, CHUNKS, step, 0)


def rows_kernel(*refs):
    got_refs = refs[:-8]
    table_ref, packed_ref, x_ref, image_ref, own_ref, send_ref, one_ref, two_ref = refs[-8:]
    freqs, channels, filters, _ = packed_ref.shape
    sources = len(got_refs)
    band_rows = got_refs[0].shape[0] // (filters + channels)
    pair = 2 * band_rows
    mine = lax.axis_index("band")
    table = jnp.concatenate([table_ref[p, mine ^ k] for p in range(2) for k in far_first(sources)], axis=0)

    def transform(start):
        block = jnp.concatenate([ref[start : start + pair, :] for ref in got_refs], axis=0)
        turned = block.T
        left = jnp.concatenate([turned[:freqs], turned[freqs:]], axis=1)
        return jnp.dot(left, table, preferred_element_type=f32)

    for j in range(filters // 2):
        both = transform(j * pair)
        x_ref[pl.ds(2 * j, freqs, stride=filters), :] = both[:, :LANES]
        x_ref[pl.ds(2 * j + 1, freqs, stride=filters), :] = both[:, LANES:]
    for c in range(channels):
        first = min(c, channels - 2)
        both = transform((filters + first) * band_rows)
        part = (c - first) * LANES
        image_ref[c * freqs : (c + 1) * freqs, :] = both[:, part : part + LANES]

    group = 8

    def step(i, carry):
        q0 = pl.multiple_of(i * group, group)
        x = x_ref[pl.ds(pl.multiple_of(q0 * filters, group * filters), group * filters), :]
        y = pltpu.roll(x, HALF, 1)
        x = x.reshape(group, filters, LANES)
        y = y.reshape(group, filters, LANES)
        one_ref[pl.ds(channels * freqs + q0, group), :] = jnp.sum(x * x, axis=1)
        for c in range(channels):
            v = packed_ref[pl.ds(q0, group), c]
            one_ref[pl.ds(c * freqs + q0, group), :] = jnp.sum(x * v, axis=1)
            two_ref[pl.ds(c * freqs + q0, group), :] = jnp.sum(y * v, axis=1)
        return carry

    lax.fori_loop(0, freqs // group, step, 0)
    top = channels * freqs
    one = one_ref[:top]
    two = two_ref[...]
    low = low_lanes(one.shape)
    cross = jnp.where(low, one - pltpu.roll(one, HALF, 1), two + pltpu.roll(two, HALF, 1))
    energy = one_ref[top:]
    energy = energy + pltpu.roll(energy, HALF, 1)
    own_ref[:top] = cross
    own_ref[top:] = energy
    send_ref[:top] = cross.astype(bf16)
    send_ref[top:] = energy.astype(bf16)


def solve_kernel(
    x_ref,
    packed_ref,
    image_ref,
    own_ref,
    peer_ref,
    inverse_ref,
    turn_ref,
    out_ref,
    rim_ref,
    re_ref,
    im_ref,
):
    freqs, channels, filters, _ = packed_ref.shape
    group = inverse_ref.shape[0] // LANES
    area = rim_ref.shape[1]
    lines = channels * filters
    top = channels * freqs
    total = own_ref[...] + peer_ref[...].astype(f32)
    denom = penalty + total[top:]
    low = low_lanes(denom.shape)
    for c in range(channels):
        span = slice(c * freqs, (c + 1) * freqs)
        coef = (image_ref[span] - total[span]) / denom
        turned = pltpu.roll(coef, HALF, 1)
        re_ref[span] = jnp.where(low, coef, -turned)
        im_ref[span] = jnp.where(low, turned, coef)

    chunk = freqs // CHUNKS
    mine = lax.axis_index("band")

    def step(i, acc):
        blocks = []
        for j in range(chunk // group):
            sides = []
            for k in range(group):
                q = i * chunk + j * group + k
                x = x_ref[pl.ds(pl.multiple_of(q * filters, filters), filters), :]
                y = pltpu.roll(x, HALF, 1)
                parts = []
                for c in range(channels):
                    d = (
                        packed_ref[q, c]
                        + x * re_ref[pl.ds(c * freqs + q, 1), :]
                        + y * im_ref[pl.ds(c * freqs + q, 1), :]
                    )
                    d = d.astype(bf16)
                    out_ref[q, 0, c] = d[:, :HALF]
                    out_ref[q, 1, c] = d[:, HALF:]
                    parts.append(d)
                sides.append(jnp.concatenate(parts, axis=0))
            blocks.append(jnp.concatenate(sides, axis=1))
        left = jnp.concatenate(blocks, axis=0)
        both = jnp.dot(left, inverse_ref[...], preferred_element_type=f32)
        for j in range(chunk // group):
            line = i * (chunk // group) + j
            part = both[j * lines : (j + 1) * lines] * turn_ref[mine, pl.ds(line, 1), :]
            acc = acc + (part[:, :area] + part[:, area:])
        return acc

    acc = lax.fori_loop(0, CHUNKS, step, jnp.zeros(rim_ref.shape, f32))
    rim_ref[...] = acc.astype(bf16)


def write_kernel(held_ref, out_ref, sem):
    copy = pltpu.make_async_copy(held_ref, out_ref, sem)
    copy.start()
    copy.wait()


def finish_kernel(*refs):
    part_refs, dual_ref, out_ref = refs[:-2], refs[-2], refs[-1]
    filters = dual_ref.shape[0]
    sums = [r[...].astype(f32) for r in part_refs]
    while len(sums) > 1:
        sums = [sums[i] + sums[i + 1] for i in range(0, len(sums), 2)]
    area = sums[0].shape[1]
    channels = sums[0].shape[0] // filters
    joined = [
        sums[0][c * filters : (c + 1) * filters] + dual_ref[:, c * area : (c + 1) * area]
        for c in range(channels)
    ]
    squares = sum(jnp.sum(w * w, axis=1, keepdims=True) for w in joined)
    spread = jnp.sqrt(squares / (channels * area))
    scale = jnp.maximum(spread, 1.0)
    for c in range(channels):
        out_ref[:, c * area : (c + 1) * area] = joined[c] / scale


def params(mib):
    return pltpu.CompilerParams(vmem_limit_bytes=mib * 1024 * 1024)


def far(array):
    return pltpu.with_memory_space_constraint(array, pltpu.HBM)


def add_kernel(a_ref, b_ref, out_ref):
    out_ref[...] = (a_ref[...].astype(f32) + b_ref[...].astype(f32)).astype(bf16)


def plain(coeff_maps, image, target, dual_rim):
    filters, band_rows, width_cols = coeff_maps.shape
    channels = image.shape[0]
    bands = lax.axis_size("band")
    height = band_rows * bands
    freqs = width_cols // bands
    table = jnp.asarray(column_table(width_cols, bands))
    stacked = jnp.concatenate([coeff_maps, image], axis=0)
    send = jnp.einsum("mrn,bnk->brmk", stacked, table, preferred_element_type=f32)
    got = lax.all_to_all(send.astype(bf16), "band", split_axis=0, concat_axis=0)
    got = got.reshape(height, filters + channels, 2, freqs)
    ramp = jnp.arange(height, dtype=jnp.int32)
    angles = (ramp[:, None] * ramp[None, :] % height).astype(f32) * (2.0 * math.pi / height)
    factor = 1.0 / math.sqrt(height)
    lookup = jnp.stack([jnp.cos(angles) * factor, jnp.sin(angles) * factor]).astype(bf16)
    both = jnp.einsum("hmpq,tgh->ptqmg", got, lookup, preferred_element_type=f32)
    re = both[0, 0] + both[1, 1]
    im = both[1, 0] - both[0, 1]
    x_re, s_re = re[:, :filters], re[:, filters:]
    x_im, s_im = im[:, :filters], im[:, filters:]
    v_re = target[:, 0].astype(f32)
    v_im = target[:, 1].astype(f32)
    energy = jnp.sum(x_re * x_re + x_im * x_im, axis=1)
    cross_re = jnp.sum(x_re[:, None] * v_re - x_im[:, None] * v_im, axis=2)
    cross_im = jnp.sum(x_re[:, None] * v_im + x_im[:, None] * v_re, axis=2)
    sums = jnp.concatenate([cross_re, cross_im, energy[:, None]], axis=1)
    sums = lax.psum(sums.astype(bf16), "filt").astype(f32)
    denom = penalty + sums[:, 2 * channels :]
    coef_re = ((s_re - sums[:, :channels]) / denom)[:, :, None]
    coef_im = ((s_im - sums[:, channels : 2 * channels]) / denom)[:, :, None]
    d_re = v_re + x_re[:, None] * coef_re + x_im[:, None] * coef_im
    d_im = v_im + x_re[:, None] * coef_im - x_im[:, None] * coef_re
    reach = jnp.arange(K, dtype=jnp.int32)
    rows = (ramp[:, None] * reach[None, :] % height).astype(f32) * (2.0 * math.pi / height)
    cols = lax.axis_index("band") * freqs + jnp.arange(freqs, dtype=jnp.int32)
    cols = (cols[:, None] * reach[None, :] % width_cols).astype(f32) * (2.0 * math.pi / width_cols)
    turn = rows[None, :, :, None] + cols[:, None, None, :]
    factor = 1.0 / math.sqrt(height * width_cols)
    exact = lax.Precision.HIGHEST
    spatial = jnp.einsum("qcmg,qgyx->mcyx", d_re, jnp.cos(turn) * factor, precision=exact)
    spatial -= jnp.einsum("qcmg,qgyx->mcyx", d_im, jnp.sin(turn) * factor, precision=exact)
    spatial = lax.psum(spatial.reshape(dual_rim.shape), "band")
    joined = spatial + dual_rim
    spread = jnp.sqrt(jnp.mean(joined * joined, axis=1, keepdims=True))
    dict_spectra = jnp.stack([d_re, d_im], axis=1).astype(bf16)
    return (dict_spectra, joined / jnp.maximum(spread, 1.0))


def body(coeff_maps, image, target, dual_rim):
    filters, band_rows, width_cols = coeff_maps.shape
    channels = image.shape[0]
    bands = lax.axis_size("band")
    height = band_rows * bands
    freqs = width_cols // bands
    rows = (filters + channels) * band_rows
    if (2 * freqs, 2 * height, 16 % band_rows, filters % 2, bands & (bands - 1)) != (LANES, LANES, 0, 0, 0):
        return plain(coeff_maps, image, target, dual_rim)

    def swap(array, k):
        return lax.ppermute(array, "band", [(i, i ^ k) for i in range(bands)])

    chunks = pl.pallas_call(
        columns_kernel,
        out_shape=(jax.ShapeDtypeStruct((rows, LANES), bf16),) * bands,
        in_specs=[pl.BlockSpec(memory_space=pltpu.HBM)] * 3,
        scratch_shapes=[
            pltpu.VMEM((rows, width_cols), bf16),
            pltpu.VMEM((2 * rows, width_cols), bf16),
            pltpu.VMEM((bands // 4, width_cols, 2 * LANES), bf16),
            pltpu.SemaphoreType.DMA((2,)),
            pltpu.SemaphoreType.DMA((bands // 2,)),
        ],
        compiler_params=params(8),
        name="columns",
    )(
        far(coeff_maps.reshape(filters * band_rows, width_cols)),
        far(image.reshape(channels * band_rows, width_cols)),
        far(jnp.asarray(column_table(width_cols, bands)[: bands // 2])),
    )
    got = [swap(chunks[k], k) if k else chunks[k] for k in far_first(bands)]

    turns = turn_table(width_cols, K, GROUP).reshape(bands, freqs // GROUP, 2 * K * K)
    packed = pl.pallas_call(
        prepare_kernel,
        out_shape=jax.ShapeDtypeStruct((freqs, channels, filters, LANES), f32),
        in_specs=[pl.BlockSpec(memory_space=pltpu.HBM)],
        scratch_shapes=[pltpu.VMEM(target.shape, bf16), pltpu.SemaphoreType.DMA((CHUNKS,))],
        compiler_params=params(12),
        name="prepare",
    )(far(target))

    lines = (channels + 1) * freqs
    x, lit, own, sums = pl.pallas_call(
        rows_kernel,
        out_shape=(
            jax.ShapeDtypeStruct((freqs * filters, LANES), f32),
            jax.ShapeDtypeStruct((channels * freqs, LANES), f32),
            jax.ShapeDtypeStruct((lines, LANES), f32),
            jax.ShapeDtypeStruct((lines, LANES), bf16),
        ),
        scratch_shapes=[
            pltpu.VMEM((lines, LANES), f32),
            pltpu.VMEM((channels * freqs, LANES), f32),
        ],
        compiler_params=params(8),
        name="rows",
    )(*got, jnp.asarray(row_table(height, band_rows)), packed)

    peer = lax.ppermute(sums, "filt", [(0, 1), (1, 0)])

    held, rim = pl.pallas_call(
        solve_kernel,
        out_shape=(
            jax.ShapeDtypeStruct(target.shape, bf16),
            jax.ShapeDtypeStruct((channels * filters, K * K), bf16),
        ),
        scratch_shapes=[
            pltpu.VMEM((channels * freqs, LANES), f32),
            pltpu.VMEM((channels * freqs, LANES), f32),
        ],
        compiler_params=params(16),
        name="solve",
    )(x, packed, lit, own, peer, jnp.asarray(inverse_table(height, width_cols, K, GROUP)), jnp.asarray(turns))

    dict_spectra = pl.pallas_call(
        write_kernel,
        out_shape=jax.ShapeDtypeStruct(target.shape, bf16),
        in_specs=[pl.BlockSpec(memory_space=pltpu.VMEM)],
        out_specs=pl.BlockSpec(memory_space=pltpu.HBM),
        scratch_shapes=[pltpu.SemaphoreType.DMA],
        compiler_params=params(4),
        name="write",
    )(held)

    near = swap(rim, 1)
    pair = pl.pallas_call(
        add_kernel,
        out_shape=jax.ShapeDtypeStruct(rim.shape, bf16),
        compiler_params=params(4),
        name="add",
    )(rim, near)
    parts = [pair] + [swap(pair, k) for k in (4, 2, 6)]
    dictionary = pl.pallas_call(
        finish_kernel,
        out_shape=jax.ShapeDtypeStruct(dual_rim.shape, f32),
        compiler_params=params(4),
        name="finish",
    )(*parts, dual_rim)
    return (dict_spectra, dictionary)


def solution(mesh):
    placed = (
        P(("grp", "filt"), "band", None),
        P("grp", "band", None),
        P(("grp", "band"), None, None, "filt", None),
        P(("grp", "filt"), None),
    )
    return jax.shard_map(
        body,
        mesh=mesh,
        in_specs=placed,
        out_specs=(P(("grp", "band"), None, None, "filt", None), P(("grp", "filt"), None)),
        check_vma=False,
    )
```

```python
import math

import jax
import jax.numpy as jnp
import numpy as np
from jax import lax
from jax.experimental import pallas as pl
from jax.experimental.pallas import tpu as pltpu
from jax.sharding import PartitionSpec as P

K = 16
LANES = 128
HALF = 64
GROUP = 4
CHUNKS = 8
BLOCKS = 4
BLOCK = 4

penalty = 1.0

bf16 = jnp.bfloat16
f32 = jnp.float32


def column_table(length, bands):
    ramp = np.arange(length)
    angles = (ramp[:, None] * ramp[None, :] % length) * (2.0 * math.pi / length)
    factor = 1.0 / math.sqrt(length)
    table = np.stack([np.cos(angles) * factor, -np.sin(angles) * factor], axis=1)
    table = table.reshape(length, 2, bands, length // bands).transpose(2, 0, 1, 3)
    return table.reshape(bands, length, 2 * length // bands).astype(np.float32).astype(bf16)


def row_table(height, band_rows):
    ramp = np.arange(height)
    angles = (ramp[:, None] * ramp[None, :] % height) * (2.0 * math.pi / height)
    factor = 1.0 / math.sqrt(height)
    cos, sin = np.cos(angles) * factor, np.sin(angles) * factor
    both = np.stack(
        [np.concatenate([cos, -sin], axis=1), np.concatenate([sin, cos], axis=1)]
    )
    both = both.reshape(2, height // band_rows, band_rows, 2 * height)
    table = np.zeros((2, height // band_rows, 2, band_rows, 2, 2 * height))
    table[:, :, 0, :, 0] = both
    table[:, :, 1, :, 1] = both
    table = table.reshape(2, height // band_rows, 2 * band_rows, 4 * height)
    return table.astype(np.float32).astype(bf16)


def inverse_table(height, columns, width, group):
    reach = np.arange(width)
    rows = (np.arange(height)[:, None] * reach[None, :] % height) * (2.0 * math.pi / height)
    cols = (np.arange(group)[:, None] * reach[None, :] % columns) * (2.0 * math.pi / columns)
    turn = rows[None, :, :, None] + cols[:, None, None, :]
    factor = 1.0 / math.sqrt(height * columns)
    cos, sin = np.cos(turn) * factor, np.sin(turn) * factor
    table = np.stack([np.stack([cos, -sin], axis=1), np.stack([-sin, -cos], axis=1)], axis=3)
    return table.reshape(group * 2 * height, 2 * width * width).astype(np.float32).astype(bf16)


def turn_table(columns, width, group):
    reach = np.arange(width)
    first = np.arange(0, columns, group)
    turn = (first[:, None] * reach[None, :] % columns) * (2.0 * math.pi / columns)
    turn = np.tile(turn, (1, width))
    return np.concatenate([np.cos(turn), np.sin(turn)], axis=1).astype(np.float32)


def far_first(bands):
    if bands == 8:
        return [7, 1, 5, 2, 3, 4, 6, 0]
    return list(range(bands - 1, -1, -1))


def low_lanes(shape):
    return lax.broadcasted_iota(jnp.int32, shape, len(shape) - 1) < HALF


def fetch_kernel(maps_ref, image_ref, table_ref, lines_ref, table_in, line_sem, table_sem):
    rows = maps_ref.shape[0]
    half = table_ref.shape[0]
    mine = lax.axis_index("band")
    copies = [
        pltpu.make_async_copy(maps_ref, lines_ref.at[:rows], line_sem.at[0]),
        pltpu.make_async_copy(image_ref, lines_ref.at[rows:], line_sem.at[1]),
    ]
    for k in range(half):
        here = table_in.at[:, k * LANES : (k + 1) * LANES]
        copies.append(pltpu.make_async_copy(table_ref.at[(mine ^ k) % half], here, table_sem.at[k]))
    for copy in copies:
        copy.start()
    for copy in copies:
        copy.wait()


def columns_kernel(lines_ref, table_ref, *out_refs):
    half = len(out_refs) // 2
    odd = lax.broadcasted_iota(jnp.int32, (1, lines_ref.shape[1]), 1) % 2
    upper = (lax.axis_index("band") >= half).astype(jnp.int32)
    near_sign = (1 - 2 * odd * upper).astype(f32).astype(bf16)
    far_sign = (1 - 2 * odd * (1 - upper)).astype(f32).astype(bf16)
    for first, sign in ((0, near_sign), (half, far_sign)):
        lines = lines_ref[...] * sign
        for k in range(0, half, 2):
            table = table_ref[:, k * LANES : (k + 2) * LANES]
            both = jnp.dot(lines, table, preferred_element_type=f32).astype(bf16)
            out_refs[first + k][...] = both[:, :LANES]
            out_refs[first + k + 1][...] = both[:, LANES:]


def prepare_kernel(target_ref, packed_ref, target_in, sems):
    freqs, _, channels, filters, height = target_ref.shape
    chunk = freqs // CHUNKS

    def fetched(i):
        span = pl.ds(i * chunk, chunk)
        return pltpu.make_async_copy(target_ref.at[span], target_in.at[span], sems.at[i])

    for i in range(CHUNKS):
        fetched(i).start()

    def step(i, carry):
        fetched(i).wait()
        for j in range(chunk):
            q = i * chunk + j
            for c in range(channels):
                packed_ref[q, c] = jnp.concatenate(
                    [target_in[q, 0, c].astype(f32), target_in[q, 1, c].astype(f32)], axis=-1
                )
        return carry

    lax.fori_loop(0, CHUNKS, step, 0)


def rows_kernel(*refs):
    got_refs = refs[:-9]
    table_ref, packed_ref, x_ref, image_ref, own_ref, send_ref, one_ref, two_ref, left_ref = refs[-9:]
    freqs, channels, filters, _ = packed_ref.shape
    sources = len(got_refs)
    band_rows = got_refs[0].shape[0] // (filters + channels)
    pair = 2 * band_rows
    mine = lax.axis_index("band")
    table = jnp.concatenate([table_ref[p, mine ^ k] for p in range(2) for k in far_first(sources)], axis=0)

    starts = [j * pair for j in range(filters // 2)]
    starts += [(filters + c) * band_rows for c in range(channels - 1)]
    for i, start in enumerate(starts):
        block = jnp.concatenate([ref[start : start + pair, :] for ref in got_refs], axis=0)
        turned = block.T
        left_ref[i * freqs : (i + 1) * freqs, :LANES] = turned[:freqs]
        left_ref[i * freqs : (i + 1) * freqs, LANES:] = turned[freqs:]
    for i in range(0, filters // 2, BLOCK):
        many = jnp.dot(
            left_ref[i * freqs : (i + BLOCK) * freqs, :], table, preferred_element_type=f32
        )
        for j in range(BLOCK):
            both = many[j * freqs : (j + 1) * freqs]
            x_ref[pl.ds(2 * (i + j), freqs, stride=filters), :] = both[:, :LANES]
            x_ref[pl.ds(2 * (i + j) + 1, freqs, stride=filters), :] = both[:, LANES:]
    many = jnp.dot(left_ref[filters // 2 * freqs :, :], table, preferred_element_type=f32)
    for c in range(channels):
        first = min(c, channels - 2)
        part = (c - first) * LANES
        image_ref[c * freqs : (c + 1) * freqs, :] = many[
            first * freqs : (first + 1) * freqs, part : part + LANES
        ]

    group = 16

    def step(i, carry):
        q0 = pl.multiple_of(i * group, group)
        x = x_ref[pl.ds(pl.multiple_of(q0 * filters, group * filters), group * filters), :]
        y = pltpu.roll(x, HALF, 1)
        x = x.reshape(group, filters, LANES)
        y = y.reshape(group, filters, LANES)
        one_ref[pl.ds(channels * freqs + q0, group), :] = jnp.sum(x * x, axis=1)
        for c in range(channels):
            v = packed_ref[pl.ds(q0, group), c]
            one_ref[pl.ds(c * freqs + q0, group), :] = jnp.sum(x * v, axis=1)
            two_ref[pl.ds(c * freqs + q0, group), :] = jnp.sum(y * v, axis=1)
        return carry

    lax.fori_loop(0, freqs // group, step, 0)
    top = channels * freqs
    one = one_ref[:top]
    two = two_ref[...]
    low = low_lanes(one.shape)
    cross = jnp.where(low, one - pltpu.roll(one, HALF, 1), two + pltpu.roll(two, HALF, 1))
    energy = one_ref[top:]
    energy = energy + pltpu.roll(energy, HALF, 1)
    own_ref[:top] = cross
    own_ref[top:] = energy
    send_ref[:top] = cross.astype(bf16)
    send_ref[top:] = energy.astype(bf16)


def solve_kernel(
    x_ref,
    packed_ref,
    image_ref,
    own_ref,
    peer_ref,
    inverse_ref,
    turn_ref,
    out_ref,
    rim_ref,
    re_ref,
    im_ref,
):
    freqs, channels, filters, _ = packed_ref.shape
    group = inverse_ref.shape[0] // LANES
    area = rim_ref.shape[1]
    lines = channels * filters
    top = channels * freqs
    total = own_ref[...] + peer_ref[...].astype(f32)
    denom = penalty + total[top:]
    low = low_lanes(denom.shape)
    for c in range(channels):
        span = slice(c * freqs, (c + 1) * freqs)
        coef = (image_ref[span] - total[span]) / denom
        turned = pltpu.roll(coef, HALF, 1)
        re_ref[span] = jnp.where(low, coef, -turned)
        im_ref[span] = jnp.where(low, turned, coef)

    chunk = freqs // BLOCKS
    mine = lax.axis_index("band")

    def step(i, acc):
        blocks = []
        for j in range(chunk // group):
            sides = []
            for k in range(group):
                q = i * chunk + j * group + k
                x = x_ref[pl.ds(pl.multiple_of(q * filters, filters), filters), :]
                y = pltpu.roll(x, HALF, 1)
                parts = []
                for c in range(channels):
                    d = (
                        packed_ref[q, c]
                        + x * re_ref[pl.ds(c * freqs + q, 1), :]
                        + y * im_ref[pl.ds(c * freqs + q, 1), :]
                    )
                    d = d.astype(bf16)
                    out_ref[q, 0, c] = d[:, :HALF]
                    out_ref[q, 1, c] = d[:, HALF:]
                    parts.append(d)
                sides.append(jnp.concatenate(parts, axis=0))
            blocks.append(jnp.concatenate(sides, axis=1))
        left = jnp.concatenate(blocks, axis=0)
        both = jnp.dot(left, inverse_ref[...], preferred_element_type=f32)
        for j in range(chunk // group):
            line = i * (chunk // group) + j
            part = both[j * lines : (j + 1) * lines] * turn_ref[mine, pl.ds(line, 1), :]
            acc = acc + (part[:, :area] + part[:, area:])
        return acc

    acc = lax.fori_loop(0, BLOCKS, step, jnp.zeros(rim_ref.shape, f32))
    rim_ref[...] = acc.astype(bf16)


def write_kernel(held_ref, out_ref, sem):
    copy = pltpu.make_async_copy(held_ref, out_ref, sem)
    copy.start()
    copy.wait()


def finish_kernel(*refs):
    part_refs, dual_ref, out_ref = refs[:-2], refs[-2], refs[-1]
    filters = dual_ref.shape[0]
    sums = [r[...].astype(f32) for r in part_refs]
    while len(sums) > 1:
        sums = [sums[i] + sums[i + 1] for i in range(0, len(sums), 2)]
    area = sums[0].shape[1]
    channels = sums[0].shape[0] // filters
    joined = [
        sums[0][c * filters : (c + 1) * filters] + dual_ref[:, c * area : (c + 1) * area]
        for c in range(channels)
    ]
    squares = sum(jnp.sum(w * w, axis=1, keepdims=True) for w in joined)
    spread = jnp.sqrt(squares / (channels * area))
    scale = jnp.maximum(spread, 1.0)
    for c in range(channels):
        out_ref[:, c * area : (c + 1) * area] = joined[c] / scale


def params(mib):
    return pltpu.CompilerParams(vmem_limit_bytes=mib * 1024 * 1024)


def far(array):
    return pltpu.with_memory_space_constraint(array, pltpu.HBM)


def add_kernel(a_ref, b_ref, out_ref):
    out_ref[...] = (a_ref[...].astype(f32) + b_ref[...].astype(f32)).astype(bf16)


def plain(coeff_maps, image, target, dual_rim):
    filters, band_rows, width_cols = coeff_maps.shape
    channels = image.shape[0]
    bands = lax.axis_size("band")
    height = band_rows * bands
    freqs = width_cols // bands
    table = jnp.asarray(column_table(width_cols, bands))
    stacked = jnp.concatenate([coeff_maps, image], axis=0)
    send = jnp.einsum("mrn,bnk->brmk", stacked, table, preferred_element_type=f32)
    got = lax.all_to_all(send.astype(bf16), "band", split_axis=0, concat_axis=0)
    got = got.reshape(height, filters + channels, 2, freqs)
    ramp = jnp.arange(height, dtype=jnp.int32)
    angles = (ramp[:, None] * ramp[None, :] % height).astype(f32) * (2.0 * math.pi / height)
    factor = 1.0 / math.sqrt(height)
    lookup = jnp.stack([jnp.cos(angles) * factor, jnp.sin(angles) * factor]).astype(bf16)
    both = jnp.einsum("hmpq,tgh->ptqmg", got, lookup, preferred_element_type=f32)
    re = both[0, 0] + both[1, 1]
    im = both[1, 0] - both[0, 1]
    x_re, s_re = re[:, :filters], re[:, filters:]
    x_im, s_im = im[:, :filters], im[:, filters:]
    v_re = target[:, 0].astype(f32)
    v_im = target[:, 1].astype(f32)
    energy = jnp.sum(x_re * x_re + x_im * x_im, axis=1)
    cross_re = jnp.sum(x_re[:, None] * v_re - x_im[:, None] * v_im, axis=2)
    cross_im = jnp.sum(x_re[:, None] * v_im + x_im[:, None] * v_re, axis=2)
    sums = jnp.concatenate([cross_re, cross_im, energy[:, None]], axis=1)
    sums = lax.psum(sums.astype(bf16), "filt").astype(f32)
    denom = penalty + sums[:, 2 * channels :]
    coef_re = ((s_re - sums[:, :channels]) / denom)[:, :, None]
    coef_im = ((s_im - sums[:, channels : 2 * channels]) / denom)[:, :, None]
    d_re = v_re + x_re[:, None] * coef_re + x_im[:, None] * coef_im
    d_im = v_im + x_re[:, None] * coef_im - x_im[:, None] * coef_re
    reach = jnp.arange(K, dtype=jnp.int32)
    rows = (ramp[:, None] * reach[None, :] % height).astype(f32) * (2.0 * math.pi / height)
    cols = lax.axis_index("band") * freqs + jnp.arange(freqs, dtype=jnp.int32)
    cols = (cols[:, None] * reach[None, :] % width_cols).astype(f32) * (2.0 * math.pi / width_cols)
    turn = rows[None, :, :, None] + cols[:, None, None, :]
    factor = 1.0 / math.sqrt(height * width_cols)
    exact = lax.Precision.HIGHEST
    spatial = jnp.einsum("qcmg,qgyx->mcyx", d_re, jnp.cos(turn) * factor, precision=exact)
    spatial -= jnp.einsum("qcmg,qgyx->mcyx", d_im, jnp.sin(turn) * factor, precision=exact)
    spatial = lax.psum(spatial.reshape(dual_rim.shape), "band")
    joined = spatial + dual_rim
    spread = jnp.sqrt(jnp.mean(joined * joined, axis=1, keepdims=True))
    dict_spectra = jnp.stack([d_re, d_im], axis=1).astype(bf16)
    return (dict_spectra, joined / jnp.maximum(spread, 1.0))


def body(coeff_maps, image, target, dual_rim):
    filters, band_rows, width_cols = coeff_maps.shape
    channels = image.shape[0]
    bands = lax.axis_size("band")
    height = band_rows * bands
    freqs = width_cols // bands
    rows = (filters + channels) * band_rows
    if (2 * freqs, 2 * height, 16 % band_rows, filters % 2, bands & (bands - 1)) != (LANES, LANES, 0, 0, 0):
        return plain(coeff_maps, image, target, dual_rim)

    def swap(array, k):
        return lax.ppermute(array, "band", [(i, i ^ k) for i in range(bands)])

    lines, table = pl.pallas_call(
        fetch_kernel,
        out_shape=(
            jax.ShapeDtypeStruct((rows, width_cols), bf16),
            jax.ShapeDtypeStruct((width_cols, bands // 2 * LANES), bf16),
        ),
        in_specs=[pl.BlockSpec(memory_space=pltpu.HBM)] * 3,
        scratch_shapes=[pltpu.SemaphoreType.DMA((2,)), pltpu.SemaphoreType.DMA((bands // 2,))],
        compiler_params=params(8),
        name="fetch",
    )(
        far(coeff_maps.reshape(filters * band_rows, width_cols)),
        far(image.reshape(channels * band_rows, width_cols)),
        far(jnp.asarray(column_table(width_cols, bands)[: bands // 2])),
    )
    chunks = pl.pallas_call(
        columns_kernel,
        out_shape=(jax.ShapeDtypeStruct((rows, LANES), bf16),) * bands,
        compiler_params=params(8),
        name="columns",
    )(lines, table)
    got = [swap(chunks[k], k) if k else chunks[k] for k in far_first(bands)]

    turns = turn_table(width_cols, K, GROUP).reshape(bands, freqs // GROUP, 2 * K * K)
    packed = pl.pallas_call(
        prepare_kernel,
        out_shape=jax.ShapeDtypeStruct((freqs, channels, filters, LANES), f32),
        in_specs=[pl.BlockSpec(memory_space=pltpu.HBM)],
        scratch_shapes=[pltpu.VMEM(target.shape, bf16), pltpu.SemaphoreType.DMA((CHUNKS,))],
        compiler_params=params(12),
        name="prepare",
    )(far(target))

    lines = (channels + 1) * freqs
    x, lit, own, sums = pl.pallas_call(
        rows_kernel,
        out_shape=(
            jax.ShapeDtypeStruct((freqs * filters, LANES), f32),
            jax.ShapeDtypeStruct((channels * freqs, LANES), f32),
            jax.ShapeDtypeStruct((lines, LANES), f32),
            jax.ShapeDtypeStruct((lines, LANES), bf16),
        ),
        scratch_shapes=[
            pltpu.VMEM((lines, LANES), f32),
            pltpu.VMEM((channels * freqs, LANES), f32),
            pltpu.VMEM(((filters // 2 + channels - 1) * freqs, 2 * LANES), bf16),
        ],
        compiler_params=params(8),
        name="rows",
    )(*got, jnp.asarray(row_table(height, band_rows)), packed)

    peer = lax.ppermute(sums, "filt", [(0, 1), (1, 0)])

    held, rim = pl.pallas_call(
        solve_kernel,
        out_shape=(
            jax.ShapeDtypeStruct(target.shape, bf16),
            jax.ShapeDtypeStruct((channels * filters, K * K), bf16),
        ),
        scratch_shapes=[
            pltpu.VMEM((channels * freqs, LANES), f32),
            pltpu.VMEM((channels * freqs, LANES), f32),
        ],
        compiler_params=params(16),
        name="solve",
    )(x, packed, lit, own, peer, jnp.asarray(inverse_table(height, width_cols, K, GROUP)), jnp.asarray(turns))

    dict_spectra = pl.pallas_call(
        write_kernel,
        out_shape=jax.ShapeDtypeStruct(target.shape, bf16),
        in_specs=[pl.BlockSpec(memory_space=pltpu.VMEM)],
        out_specs=pl.BlockSpec(memory_space=pltpu.HBM),
        scratch_shapes=[pltpu.SemaphoreType.DMA],
        compiler_params=params(4),
        name="write",
    )(held)

    near = swap(rim, 1)
    pair = pl.pallas_call(
        add_kernel,
        out_shape=jax.ShapeDtypeStruct(rim.shape, bf16),
        compiler_params=params(4),
        name="add",
    )(rim, near)
    parts = [pair] + [swap(pair, k) for k in (4, 2, 6)]
    dictionary = pl.pallas_call(
        finish_kernel,
        out_shape=jax.ShapeDtypeStruct(dual_rim.shape, f32),
        compiler_params=params(4),
        name="finish",
    )(*parts, dual_rim)
    return (dict_spectra, dictionary)


def solution(mesh):
    placed = (
        P(("grp", "filt"), "band", None),
        P("grp", "band", None),
        P(("grp", "band"), None, None, "filt", None),
        P(("grp", "filt"), None),
    )
    return jax.shard_map(
        body,
        mesh=mesh,
        in_specs=placed,
        out_specs=(P(("grp", "band"), None, None, "filt", None), P(("grp", "filt"), None)),
        check_vma=False,
    )
```

```python
import math

import jax
import jax.numpy as jnp
import numpy as np
from jax import lax
from jax.experimental import pallas as pl
from jax.experimental.pallas import tpu as pltpu
from jax.sharding import PartitionSpec as P

K = 16
LANES = 128
HALF = 64
GROUP = 4
CHUNKS = 8
BLOCKS = 4
BLOCK = 4

penalty = 1.0

bf16 = jnp.bfloat16
f32 = jnp.float32


def column_table(length, bands):
    ramp = np.arange(length)
    angles = (ramp[:, None] * ramp[None, :] % length) * (2.0 * math.pi / length)
    factor = 1.0 / math.sqrt(length)
    table = np.stack([np.cos(angles) * factor, -np.sin(angles) * factor], axis=1)
    table = table.reshape(length, 2, bands, length // bands).transpose(2, 0, 1, 3)
    return table.reshape(bands, length, 2 * length // bands).astype(np.float32).astype(bf16)


def row_table(height, band_rows):
    ramp = np.arange(height)
    angles = (ramp[:, None] * ramp[None, :] % height) * (2.0 * math.pi / height)
    factor = 1.0 / math.sqrt(height)
    cos, sin = np.cos(angles) * factor, np.sin(angles) * factor
    both = np.stack(
        [np.concatenate([cos, -sin], axis=1), np.concatenate([sin, cos], axis=1)]
    )
    both = both.reshape(2, height // band_rows, band_rows, 2 * height)
    table = np.zeros((2, height // band_rows, 2, band_rows, 2, 2 * height))
    table[:, :, 0, :, 0] = both
    table[:, :, 1, :, 1] = both
    table = table.reshape(2, height // band_rows, 2 * band_rows, 4 * height)
    return table.astype(np.float32).astype(bf16)


def inverse_table(height, columns, width, group):
    reach = np.arange(width)
    rows = (np.arange(height)[:, None] * reach[None, :] % height) * (2.0 * math.pi / height)
    cols = (np.arange(group)[:, None] * reach[None, :] % columns) * (2.0 * math.pi / columns)
    turn = rows[None, :, :, None] + cols[:, None, None, :]
    factor = 1.0 / math.sqrt(height * columns)
    cos, sin = np.cos(turn) * factor, np.sin(turn) * factor
    table = np.stack([np.stack([cos, -sin], axis=1), np.stack([-sin, -cos], axis=1)], axis=3)
    return table.reshape(group * 2 * height, 2 * width * width).astype(np.float32).astype(bf16)


def turn_table(columns, width, group):
    reach = np.arange(width)
    first = np.arange(0, columns, group)
    turn = (first[:, None] * reach[None, :] % columns) * (2.0 * math.pi / columns)
    turn = np.tile(turn, (1, width))
    return np.concatenate([np.cos(turn), np.sin(turn)], axis=1).astype(np.float32)


def far_first(bands):
    if bands == 8:
        return [7, 1, 5, 2, 3, 4, 6, 0]
    return list(range(bands - 1, -1, -1))


def low_lanes(shape):
    return lax.broadcasted_iota(jnp.int32, shape, len(shape) - 1) < HALF


def fetch_kernel(maps_ref, image_ref, table_ref, lines_ref, table_in, line_sem, table_sem):
    rows = maps_ref.shape[0]
    first = lax.axis_index("filt") * (rows + image_ref.shape[0] - lines_ref.shape[0])
    half = table_ref.shape[0]
    mine = lax.axis_index("band")
    copies = [
        pltpu.make_async_copy(maps_ref, lines_ref.at[:rows], line_sem.at[0]),
        pltpu.make_async_copy(
            image_ref.at[pl.ds(pl.multiple_of(first, 8), lines_ref.shape[0] - rows)],
            lines_ref.at[rows:],
            line_sem.at[1],
        ),
    ]
    for k in range(half):
        here = table_in.at[:, k * LANES : (k + 1) * LANES]
        copies.append(pltpu.make_async_copy(table_ref.at[(mine ^ k) % half], here, table_sem.at[k]))
    for copy in copies:
        copy.start()
    for copy in copies:
        copy.wait()


def columns_kernel(lines_ref, table_ref, *out_refs):
    half = len(out_refs) // 2
    odd = lax.broadcasted_iota(jnp.int32, (1, lines_ref.shape[1]), 1) % 2
    upper = (lax.axis_index("band") >= half).astype(jnp.int32)
    near_sign = (1 - 2 * odd * upper).astype(f32).astype(bf16)
    far_sign = (1 - 2 * odd * (1 - upper)).astype(f32).astype(bf16)
    for first, sign in ((0, near_sign), (half, far_sign)):
        lines = lines_ref[...] * sign
        for k in range(0, half, 2):
            table = table_ref[:, k * LANES : (k + 2) * LANES]
            both = jnp.dot(lines, table, preferred_element_type=f32).astype(bf16)
            out_refs[first + k][...] = both[:, :LANES]
            out_refs[first + k + 1][...] = both[:, LANES:]


def prepare_kernel(target_ref, packed_ref, target_in, sems):
    freqs, _, channels, filters, height = target_ref.shape
    chunk = freqs // CHUNKS

    def fetched(i):
        span = pl.ds(i * chunk, chunk)
        return pltpu.make_async_copy(target_ref.at[span], target_in.at[span], sems.at[i])

    for i in range(CHUNKS):
        fetched(i).start()

    def step(i, carry):
        fetched(i).wait()
        for j in range(chunk):
            q = i * chunk + j
            for c in range(channels):
                packed_ref[q, c] = jnp.concatenate(
                    [target_in[q, 0, c].astype(f32), target_in[q, 1, c].astype(f32)], axis=-1
                )
        return carry

    lax.fori_loop(0, CHUNKS, step, 0)


def rows_kernel(*refs):
    got_refs = refs[:-9]
    table_ref, packed_ref, x_ref, own_ref, send_ref, one_ref, two_ref, lit_ref, left_ref = refs[-9:]
    freqs, channels, filters, _ = packed_ref.shape
    sources = len(got_refs)
    band_rows = got_refs[0].shape[0] // (filters + channels - 1)
    pair = 2 * band_rows
    mine = lax.axis_index("band")
    table = jnp.concatenate([table_ref[p, mine ^ k] for p in range(2) for k in far_first(sources)], axis=0)

    starts = [j * pair for j in range(filters // 2)]
    starts += [(filters + c) * band_rows for c in range(channels - 2)]
    for i, start in enumerate(starts):
        block = jnp.concatenate([ref[start : start + pair, :] for ref in got_refs], axis=0)
        turned = block.T
        left_ref[i * freqs : (i + 1) * freqs, :LANES] = turned[:freqs]
        left_ref[i * freqs : (i + 1) * freqs, LANES:] = turned[freqs:]
    for i in range(0, filters // 2, BLOCK):
        many = jnp.dot(
            left_ref[i * freqs : (i + BLOCK) * freqs, :], table, preferred_element_type=f32
        )
        for j in range(BLOCK):
            both = many[j * freqs : (j + 1) * freqs]
            x_ref[pl.ds(2 * (i + j), freqs, stride=filters), :] = both[:, :LANES]
            x_ref[pl.ds(2 * (i + j) + 1, freqs, stride=filters), :] = both[:, LANES:]
    many = jnp.dot(left_ref[filters // 2 * freqs :, :], table, preferred_element_type=f32)
    held = [many[:freqs, :LANES]]
    for c in range(channels - 2):
        held.append(many[c * freqs : (c + 1) * freqs, LANES:])
    core = lax.axis_index("filt").astype(f32)
    for c in range(channels):
        share = 1.0 if c in (0, channels - 1) else 0.5
        lit = jnp.zeros((freqs, LANES), f32)
        if c < channels - 1:
            lit = lit + held[c] * (share * (1.0 - core))
        if c > 0:
            lit = lit + held[c - 1] * (share * core)
        lit_ref[c * freqs : (c + 1) * freqs, :] = lit

    group = 16

    def step(i, carry):
        q0 = pl.multiple_of(i * group, group)
        x = x_ref[pl.ds(pl.multiple_of(q0 * filters, group * filters), group * filters), :]
        y = pltpu.roll(x, HALF, 1)
        x = x.reshape(group, filters, LANES)
        y = y.reshape(group, filters, LANES)
        one_ref[pl.ds(channels * freqs + q0, group), :] = jnp.sum(x * x, axis=1)
        for c in range(channels):
            v = packed_ref[pl.ds(q0, group), c]
            one_ref[pl.ds(c * freqs + q0, group), :] = jnp.sum(x * v, axis=1)
            two_ref[pl.ds(c * freqs + q0, group), :] = jnp.sum(y * v, axis=1)
        return carry

    lax.fori_loop(0, freqs // group, step, 0)
    top = channels * freqs
    one = one_ref[:top]
    two = two_ref[...]
    low = low_lanes(one.shape)
    cross = jnp.where(low, one - pltpu.roll(one, HALF, 1), two + pltpu.roll(two, HALF, 1))
    cross = lit_ref[...] - cross
    energy = one_ref[top:]
    energy = energy + pltpu.roll(energy, HALF, 1)
    own_ref[:top] = cross
    own_ref[top:] = energy
    send_ref[:top] = cross.astype(bf16)
    send_ref[top:] = energy.astype(bf16)


def solve_kernel(
    x_ref,
    packed_ref,
    own_ref,
    peer_ref,
    inverse_ref,
    turn_ref,
    out_ref,
    rim_ref,
    re_ref,
    im_ref,
):
    freqs, channels, filters, _ = packed_ref.shape
    group = inverse_ref.shape[0] // LANES
    area = rim_ref.shape[1]
    lines = channels * filters
    top = channels * freqs
    total = own_ref[...] + peer_ref[...].astype(f32)
    denom = penalty + total[top:]
    low = low_lanes(denom.shape)
    for c in range(channels):
        span = slice(c * freqs, (c + 1) * freqs)
        coef = total[span] / denom
        turned = pltpu.roll(coef, HALF, 1)
        re_ref[span] = jnp.where(low, coef, -turned)
        im_ref[span] = jnp.where(low, turned, coef)

    chunk = freqs // BLOCKS
    mine = lax.axis_index("band")

    def step(i, acc):
        blocks = []
        for j in range(chunk // group):
            sides = []
            for k in range(group):
                q = i * chunk + j * group + k
                x = x_ref[pl.ds(pl.multiple_of(q * filters, filters), filters), :]
                y = pltpu.roll(x, HALF, 1)
                parts = []
                for c in range(channels):
                    d = (
                        packed_ref[q, c]
                        + x * re_ref[pl.ds(c * freqs + q, 1), :]
                        + y * im_ref[pl.ds(c * freqs + q, 1), :]
                    )
                    d = d.astype(bf16)
                    out_ref[q, 0, c] = d[:, :HALF]
                    out_ref[q, 1, c] = d[:, HALF:]
                    parts.append(d)
                sides.append(jnp.concatenate(parts, axis=0))
            blocks.append(jnp.concatenate(sides, axis=1))
        left = jnp.concatenate(blocks, axis=0)
        both = jnp.dot(left, inverse_ref[...], preferred_element_type=f32)
        for j in range(chunk // group):
            line = i * (chunk // group) + j
            part = both[j * lines : (j + 1) * lines] * turn_ref[mine, pl.ds(line, 1), :]
            acc = acc + (part[:, :area] + part[:, area:])
        return acc

    acc = lax.fori_loop(0, BLOCKS, step, jnp.zeros(rim_ref.shape, f32))
    rim_ref[...] = acc.astype(bf16)


def write_kernel(held_ref, out_ref, sem):
    copy = pltpu.make_async_copy(held_ref, out_ref, sem)
    copy.start()
    copy.wait()


def finish_kernel(*refs):
    part_refs, dual_ref, out_ref = refs[:-2], refs[-2], refs[-1]
    filters = dual_ref.shape[0]
    sums = [r[...].astype(f32) for r in part_refs]
    while len(sums) > 1:
        sums = [sums[i] + sums[i + 1] for i in range(0, len(sums), 2)]
    area = sums[0].shape[1]
    channels = sums[0].shape[0] // filters
    joined = [
        sums[0][c * filters : (c + 1) * filters] + dual_ref[:, c * area : (c + 1) * area]
        for c in range(channels)
    ]
    squares = sum(jnp.sum(w * w, axis=1, keepdims=True) for w in joined)
    spread = jnp.sqrt(squares / (channels * area))
    scale = jnp.maximum(spread, 1.0)
    for c in range(channels):
        out_ref[:, c * area : (c + 1) * area] = joined[c] / scale


def params(mib):
    return pltpu.CompilerParams(vmem_limit_bytes=mib * 1024 * 1024)


def far(array):
    return pltpu.with_memory_space_constraint(array, pltpu.HBM)


def add_kernel(a_ref, b_ref, out_ref):
    out_ref[...] = (a_ref[...].astype(f32) + b_ref[...].astype(f32)).astype(bf16)


def plain(coeff_maps, image, target, dual_rim):
    filters, band_rows, width_cols = coeff_maps.shape
    channels = image.shape[0]
    bands = lax.axis_size("band")
    height = band_rows * bands
    freqs = width_cols // bands
    table = jnp.asarray(column_table(width_cols, bands))
    stacked = jnp.concatenate([coeff_maps, image], axis=0)
    send = jnp.einsum("mrn,bnk->brmk", stacked, table, preferred_element_type=f32)
    got = lax.all_to_all(send.astype(bf16), "band", split_axis=0, concat_axis=0)
    got = got.reshape(height, filters + channels, 2, freqs)
    ramp = jnp.arange(height, dtype=jnp.int32)
    angles = (ramp[:, None] * ramp[None, :] % height).astype(f32) * (2.0 * math.pi / height)
    factor = 1.0 / math.sqrt(height)
    lookup = jnp.stack([jnp.cos(angles) * factor, jnp.sin(angles) * factor]).astype(bf16)
    both = jnp.einsum("hmpq,tgh->ptqmg", got, lookup, preferred_element_type=f32)
    re = both[0, 0] + both[1, 1]
    im = both[1, 0] - both[0, 1]
    x_re, s_re = re[:, :filters], re[:, filters:]
    x_im, s_im = im[:, :filters], im[:, filters:]
    v_re = target[:, 0].astype(f32)
    v_im = target[:, 1].astype(f32)
    energy = jnp.sum(x_re * x_re + x_im * x_im, axis=1)
    cross_re = jnp.sum(x_re[:, None] * v_re - x_im[:, None] * v_im, axis=2)
    cross_im = jnp.sum(x_re[:, None] * v_im + x_im[:, None] * v_re, axis=2)
    sums = jnp.concatenate([cross_re, cross_im, energy[:, None]], axis=1)
    sums = lax.psum(sums.astype(bf16), "filt").astype(f32)
    denom = penalty + sums[:, 2 * channels :]
    coef_re = ((s_re - sums[:, :channels]) / denom)[:, :, None]
    coef_im = ((s_im - sums[:, channels : 2 * channels]) / denom)[:, :, None]
    d_re = v_re + x_re[:, None] * coef_re + x_im[:, None] * coef_im
    d_im = v_im + x_re[:, None] * coef_im - x_im[:, None] * coef_re
    reach = jnp.arange(K, dtype=jnp.int32)
    rows = (ramp[:, None] * reach[None, :] % height).astype(f32) * (2.0 * math.pi / height)
    cols = lax.axis_index("band") * freqs + jnp.arange(freqs, dtype=jnp.int32)
    cols = (cols[:, None] * reach[None, :] % width_cols).astype(f32) * (2.0 * math.pi / width_cols)
    turn = rows[None, :, :, None] + cols[:, None, None, :]
    factor = 1.0 / math.sqrt(height * width_cols)
    exact = lax.Precision.HIGHEST
    spatial = jnp.einsum("qcmg,qgyx->mcyx", d_re, jnp.cos(turn) * factor, precision=exact)
    spatial -= jnp.einsum("qcmg,qgyx->mcyx", d_im, jnp.sin(turn) * factor, precision=exact)
    spatial = lax.psum(spatial.reshape(dual_rim.shape), "band")
    joined = spatial + dual_rim
    spread = jnp.sqrt(jnp.mean(joined * joined, axis=1, keepdims=True))
    dict_spectra = jnp.stack([d_re, d_im], axis=1).astype(bf16)
    return (dict_spectra, joined / jnp.maximum(spread, 1.0))


def body(coeff_maps, image, target, dual_rim):
    filters, band_rows, width_cols = coeff_maps.shape
    channels = image.shape[0]
    bands = lax.axis_size("band")
    height = band_rows * bands
    freqs = width_cols // bands
    rows = (filters + channels - 1) * band_rows
    cores = lax.axis_size("filt")
    fits = (2 * freqs, 2 * height, band_rows, channels, filters % 2, bands & (bands - 1), cores)
    if fits != (LANES, LANES, 8, 3, 0, 0, 2):
        return plain(coeff_maps, image, target, dual_rim)

    def swap(array, k):
        return lax.ppermute(array, "band", [(i, i ^ k) for i in range(bands)])

    lines, table = pl.pallas_call(
        fetch_kernel,
        out_shape=(
            jax.ShapeDtypeStruct((rows, width_cols), bf16),
            jax.ShapeDtypeStruct((width_cols, bands // 2 * LANES), bf16),
        ),
        in_specs=[pl.BlockSpec(memory_space=pltpu.HBM)] * 3,
        scratch_shapes=[pltpu.SemaphoreType.DMA((2,)), pltpu.SemaphoreType.DMA((bands // 2,))],
        compiler_params=params(8),
        name="fetch",
    )(
        far(coeff_maps.reshape(filters * band_rows, width_cols)),
        far(image.reshape(channels * band_rows, width_cols)),
        far(jnp.asarray(column_table(width_cols, bands)[: bands // 2])),
    )
    chunks = pl.pallas_call(
        columns_kernel,
        out_shape=(jax.ShapeDtypeStruct((rows, LANES), bf16),) * bands,
        compiler_params=params(8),
        name="columns",
    )(lines, table)
    got = [swap(chunks[k], k) if k else chunks[k] for k in far_first(bands)]

    turns = turn_table(width_cols, K, GROUP).reshape(bands, freqs // GROUP, 2 * K * K)
    packed = pl.pallas_call(
        prepare_kernel,
        out_shape=jax.ShapeDtypeStruct((freqs, channels, filters, LANES), f32),
        in_specs=[pl.BlockSpec(memory_space=pltpu.HBM)],
        scratch_shapes=[pltpu.VMEM(target.shape, bf16), pltpu.SemaphoreType.DMA((CHUNKS,))],
        compiler_params=params(12),
        name="prepare",
    )(far(target))

    lines = (channels + 1) * freqs
    x, own, sums = pl.pallas_call(
        rows_kernel,
        out_shape=(
            jax.ShapeDtypeStruct((freqs * filters, LANES), f32),
            jax.ShapeDtypeStruct((lines, LANES), f32),
            jax.ShapeDtypeStruct((lines, LANES), bf16),
        ),
        scratch_shapes=[
            pltpu.VMEM((lines, LANES), f32),
            pltpu.VMEM((channels * freqs, LANES), f32),
            pltpu.VMEM((channels * freqs, LANES), f32),
            pltpu.VMEM(((filters // 2 + channels - 2) * freqs, 2 * LANES), bf16),
        ],
        compiler_params=params(8),
        name="rows",
    )(*got, jnp.asarray(row_table(height, band_rows)), packed)

    peer = lax.ppermute(sums, "filt", [(0, 1), (1, 0)])

    held, rim = pl.pallas_call(
        solve_kernel,
        out_shape=(
            jax.ShapeDtypeStruct(target.shape, bf16),
            jax.ShapeDtypeStruct((channels * filters, K * K), bf16),
        ),
        scratch_shapes=[
            pltpu.VMEM((channels * freqs, LANES), f32),
            pltpu.VMEM((channels * freqs, LANES), f32),
        ],
        compiler_params=params(16),
        name="solve",
    )(x, packed, own, peer, jnp.asarray(inverse_table(height, width_cols, K, GROUP)), jnp.asarray(turns))

    dict_spectra = pl.pallas_call(
        write_kernel,
        out_shape=jax.ShapeDtypeStruct(target.shape, bf16),
        in_specs=[pl.BlockSpec(memory_space=pltpu.VMEM)],
        out_specs=pl.BlockSpec(memory_space=pltpu.HBM),
        scratch_shapes=[pltpu.SemaphoreType.DMA],
        compiler_params=params(4),
        name="write",
    )(held)

    near = swap(rim, 1)
    pair = pl.pallas_call(
        add_kernel,
        out_shape=jax.ShapeDtypeStruct(rim.shape, bf16),
        compiler_params=params(4),
        name="add",
    )(rim, near)
    parts = [pair] + [swap(pair, k) for k in (4, 2, 6)]
    dictionary = pl.pallas_call(
        finish_kernel,
        out_shape=jax.ShapeDtypeStruct(dual_rim.shape, f32),
        compiler_params=params(4),
        name="finish",
    )(*parts, dual_rim)
    return (dict_spectra, dictionary)


def solution(mesh):
    placed = (
        P(("grp", "filt"), "band", None),
        P("grp", "band", None),
        P(("grp", "band"), None, None, "filt", None),
        P(("grp", "filt"), None),
    )
    return jax.shard_map(
        body,
        mesh=mesh,
        in_specs=placed,
        out_specs=(P(("grp", "band"), None, None, "filt", None), P(("grp", "filt"), None)),
        check_vma=False,
    )
```

```python
import math

import jax
import jax.numpy as jnp
import numpy as np
from jax import lax
from jax.experimental import pallas as pl
from jax.experimental.pallas import tpu as pltpu
from jax.sharding import PartitionSpec as P

K = 16
LANES = 128
HALF = 64
GROUP = 2
CHUNKS = 8
BLOCKS = 4
BLOCK = 4

penalty = 1.0

bf16 = jnp.bfloat16
f32 = jnp.float32


def column_table(length, bands):
    ramp = np.arange(length)
    angles = (ramp[:, None] * ramp[None, :] % length) * (2.0 * math.pi / length)
    factor = 1.0 / math.sqrt(length)
    table = np.stack([np.cos(angles) * factor, -np.sin(angles) * factor], axis=1)
    table = table.reshape(length, 2, bands, length // bands).transpose(2, 0, 1, 3)
    return table.reshape(bands, length, 2 * length // bands).astype(np.float32).astype(bf16)


def row_table(height, band_rows):
    ramp = np.arange(height)
    angles = (ramp[:, None] * ramp[None, :] % height) * (2.0 * math.pi / height)
    factor = 1.0 / math.sqrt(height)
    cos, sin = np.cos(angles) * factor, np.sin(angles) * factor
    both = np.stack(
        [np.concatenate([cos, -sin], axis=1), np.concatenate([sin, cos], axis=1)]
    )
    both = both.reshape(2, height // band_rows, band_rows, 2 * height)
    table = np.zeros((2, height // band_rows, 2, band_rows, 2, 2 * height))
    table[:, :, 0, :, 0] = both
    table[:, :, 1, :, 1] = both
    table = table.reshape(2, height // band_rows, 2 * band_rows, 4 * height)
    return table.astype(np.float32).astype(bf16)


def inverse_table(height, columns, width, group):
    reach = np.arange(width)
    rows = (np.arange(height)[:, None] * reach[None, :] % height) * (2.0 * math.pi / height)
    cols = (np.arange(group)[:, None] * reach[None, :] % columns) * (2.0 * math.pi / columns)
    turn = rows[None, :, :, None] + cols[:, None, None, :]
    factor = 1.0 / math.sqrt(height * columns)
    cos, sin = np.cos(turn) * factor, np.sin(turn) * factor
    table = np.stack([np.stack([cos, -sin], axis=1), np.stack([-sin, -cos], axis=1)], axis=3)
    return table.reshape(group * 2 * height, 2 * width * width).astype(np.float32).astype(bf16)


def turn_table(columns, width, group):
    reach = np.arange(width)
    first = np.arange(0, columns, group)
    turn = (first[:, None] * reach[None, :] % columns) * (2.0 * math.pi / columns)
    turn = np.tile(turn, (1, width))
    return np.concatenate([np.cos(turn), np.sin(turn)], axis=1).astype(np.float32)


def far_first(bands):
    if bands == 8:
        return [7, 1, 5, 2, 3, 4, 6, 0]
    return list(range(bands - 1, -1, -1))


def low_lanes(shape):
    return lax.broadcasted_iota(jnp.int32, shape, len(shape) - 1) < HALF


def fetch_kernel(maps_ref, image_ref, table_ref, lines_ref, table_in, line_sem, table_sem):
    rows = maps_ref.shape[0]
    first = lax.axis_index("filt") * (rows + image_ref.shape[0] - lines_ref.shape[0])
    half = table_ref.shape[0]
    mine = lax.axis_index("band")
    copies = [
        pltpu.make_async_copy(maps_ref, lines_ref.at[:rows], line_sem.at[0]),
        pltpu.make_async_copy(
            image_ref.at[pl.ds(pl.multiple_of(first, 8), lines_ref.shape[0] - rows)],
            lines_ref.at[rows:],
            line_sem.at[1],
        ),
    ]
    for k in range(half):
        here = table_in.at[:, k * LANES : (k + 1) * LANES]
        copies.append(pltpu.make_async_copy(table_ref.at[(mine ^ k) % half], here, table_sem.at[k]))
    for copy in copies:
        copy.start()
    for copy in copies:
        copy.wait()


def columns_kernel(lines_ref, table_ref, *out_refs):
    half = len(out_refs) // 2
    odd = lax.broadcasted_iota(jnp.int32, (1, lines_ref.shape[1]), 1) % 2
    upper = (lax.axis_index("band") >= half).astype(jnp.int32)
    near_sign = (1 - 2 * odd * upper).astype(f32).astype(bf16)
    far_sign = (1 - 2 * odd * (1 - upper)).astype(f32).astype(bf16)
    for first, sign in ((0, near_sign), (half, far_sign)):
        lines = lines_ref[...] * sign
        for k in range(0, half, 2):
            table = table_ref[:, k * LANES : (k + 2) * LANES]
            both = jnp.dot(lines, table, preferred_element_type=f32).astype(bf16)
            out_refs[first + k][...] = both[:, :LANES]
            out_refs[first + k + 1][...] = both[:, LANES:]


def prepare_kernel(target_ref, packed_ref, target_in, sems):
    freqs, _, channels, filters, height = target_ref.shape
    chunk = freqs // CHUNKS

    def fetched(i):
        span = pl.ds(i * chunk, chunk)
        return pltpu.make_async_copy(target_ref.at[span], target_in.at[span], sems.at[i])

    for i in range(CHUNKS):
        fetched(i).start()

    def step(i, carry):
        fetched(i).wait()
        for j in range(chunk):
            q = i * chunk + j
            for c in range(channels):
                packed_ref[q, c] = jnp.concatenate(
                    [target_in[q, 0, c].astype(f32), target_in[q, 1, c].astype(f32)], axis=-1
                )
        return carry

    lax.fori_loop(0, CHUNKS, step, 0)


def rows_kernel(*refs):
    got_refs = refs[:-9]
    table_ref, packed_ref, x_ref, own_ref, send_ref, one_ref, two_ref, lit_ref, left_ref = refs[-9:]
    freqs, channels, filters, _ = packed_ref.shape
    sources = len(got_refs)
    band_rows = got_refs[0].shape[0] // (filters + channels - 1)
    pair = 2 * band_rows
    mine = lax.axis_index("band")
    table = jnp.concatenate([table_ref[p, mine ^ k] for p in range(2) for k in far_first(sources)], axis=0)

    starts = [j * pair for j in range(filters // 2)]
    starts += [(filters + c) * band_rows for c in range(channels - 2)]
    for i, start in enumerate(starts):
        block = jnp.concatenate([ref[start : start + pair, :] for ref in got_refs], axis=0)
        turned = block.T
        left_ref[i * freqs : (i + 1) * freqs, :LANES] = turned[:freqs]
        left_ref[i * freqs : (i + 1) * freqs, LANES:] = turned[freqs:]
    for i in range(0, filters // 2, BLOCK):
        many = jnp.dot(
            left_ref[i * freqs : (i + BLOCK) * freqs, :], table, preferred_element_type=f32
        )
        for j in range(BLOCK):
            both = many[j * freqs : (j + 1) * freqs]
            x_ref[pl.ds(2 * (i + j), freqs, stride=filters), :] = both[:, :LANES]
            x_ref[pl.ds(2 * (i + j) + 1, freqs, stride=filters), :] = both[:, LANES:]
    many = jnp.dot(left_ref[filters // 2 * freqs :, :], table, preferred_element_type=f32)
    held = [many[:freqs, :LANES]]
    for c in range(channels - 2):
        held.append(many[c * freqs : (c + 1) * freqs, LANES:])
    core = lax.axis_index("filt").astype(f32)
    for c in range(channels):
        share = 1.0 if c in (0, channels - 1) else 0.5
        lit = jnp.zeros((freqs, LANES), f32)
        if c < channels - 1:
            lit = lit + held[c] * (share * (1.0 - core))
        if c > 0:
            lit = lit + held[c - 1] * (share * core)
        lit_ref[c * freqs : (c + 1) * freqs, :] = lit

    group = 16

    def step(i, carry):
        q0 = pl.multiple_of(i * group, group)
        x = x_ref[pl.ds(pl.multiple_of(q0 * filters, group * filters), group * filters), :]
        y = pltpu.roll(x, HALF, 1)
        x = x.reshape(group, filters, LANES)
        y = y.reshape(group, filters, LANES)
        one_ref[pl.ds(channels * freqs + q0, group), :] = jnp.sum(x * x, axis=1)
        for c in range(channels):
            v = packed_ref[pl.ds(q0, group), c]
            one_ref[pl.ds(c * freqs + q0, group), :] = jnp.sum(x * v, axis=1)
            two_ref[pl.ds(c * freqs + q0, group), :] = jnp.sum(y * v, axis=1)
        return carry

    lax.fori_loop(0, freqs // group, step, 0)
    top = channels * freqs
    one = one_ref[:top]
    two = two_ref[...]
    low = low_lanes(one.shape)
    cross = jnp.where(low, one - pltpu.roll(one, HALF, 1), two + pltpu.roll(two, HALF, 1))
    cross = lit_ref[...] - cross
    energy = one_ref[top:]
    energy = energy + pltpu.roll(energy, HALF, 1)
    own_ref[:top] = cross
    own_ref[top:] = energy
    send_ref[:top] = cross.astype(bf16)
    send_ref[top:] = energy.astype(bf16)


def solve_kernel(
    x_ref,
    packed_ref,
    own_ref,
    peer_ref,
    inverse_ref,
    turn_ref,
    out_ref,
    rim_ref,
    re_ref,
    im_ref,
):
    freqs, channels, filters, _ = packed_ref.shape
    group = inverse_ref.shape[0] // LANES
    area = rim_ref.shape[1]
    lines = channels * filters
    top = channels * freqs
    total = own_ref[...] + peer_ref[...].astype(f32)
    denom = penalty + total[top:]
    low = low_lanes(denom.shape)
    for c in range(channels):
        span = slice(c * freqs, (c + 1) * freqs)
        coef = total[span] / denom
        turned = pltpu.roll(coef, HALF, 1)
        re_ref[span] = jnp.where(low, coef, -turned)
        im_ref[span] = jnp.where(low, turned, coef)

    chunk = freqs // BLOCKS
    mine = lax.axis_index("band")

    def step(i, acc):
        blocks = []
        for j in range(chunk // group):
            sides = []
            for k in range(group):
                q = i * chunk + j * group + k
                x = x_ref[pl.ds(pl.multiple_of(q * filters, filters), filters), :]
                y = pltpu.roll(x, HALF, 1)
                parts = []
                for c in range(channels):
                    d = (
                        packed_ref[q, c]
                        + x * re_ref[pl.ds(c * freqs + q, 1), :]
                        + y * im_ref[pl.ds(c * freqs + q, 1), :]
                    )
                    d = d.astype(bf16)
                    out_ref[q, 0, c] = d[:, :HALF]
                    out_ref[q, 1, c] = d[:, HALF:]
                    parts.append(d)
                sides.append(jnp.concatenate(parts, axis=0))
            blocks.append(jnp.concatenate(sides, axis=1))
        left = jnp.concatenate(blocks, axis=0)
        both = jnp.dot(left, inverse_ref[...], preferred_element_type=f32)
        for j in range(chunk // group):
            line = i * (chunk // group) + j
            part = both[j * lines : (j + 1) * lines] * turn_ref[mine, pl.ds(line, 1), :]
            acc = acc + (part[:, :area] + part[:, area:])
        return acc

    acc = lax.fori_loop(0, BLOCKS, step, jnp.zeros(rim_ref.shape, f32))
    rim_ref[...] = acc.astype(bf16)


def write_kernel(held_ref, out_ref, sem):
    copy = pltpu.make_async_copy(held_ref, out_ref, sem)
    copy.start()
    copy.wait()


def finish_kernel(*refs):
    part_refs, dual_ref, out_ref = refs[:-2], refs[-2], refs[-1]
    filters = dual_ref.shape[0]
    sums = [r[...].astype(f32) for r in part_refs]
    while len(sums) > 1:
        sums = [sums[i] + sums[i + 1] for i in range(0, len(sums), 2)]
    area = sums[0].shape[1]
    channels = sums[0].shape[0] // filters
    joined = [
        sums[0][c * filters : (c + 1) * filters] + dual_ref[:, c * area : (c + 1) * area]
        for c in range(channels)
    ]
    squares = sum(jnp.sum(w * w, axis=1, keepdims=True) for w in joined)
    spread = jnp.sqrt(squares / (channels * area))
    scale = jnp.maximum(spread, 1.0)
    for c in range(channels):
        out_ref[:, c * area : (c + 1) * area] = joined[c] / scale


def params(mib):
    return pltpu.CompilerParams(vmem_limit_bytes=mib * 1024 * 1024)


def far(array):
    return pltpu.with_memory_space_constraint(array, pltpu.HBM)


def add_kernel(a_ref, b_ref, out_ref):
    out_ref[...] = (a_ref[...].astype(f32) + b_ref[...].astype(f32)).astype(bf16)


def plain(coeff_maps, image, target, dual_rim):
    filters, band_rows, width_cols = coeff_maps.shape
    channels = image.shape[0]
    bands = lax.axis_size("band")
    height = band_rows * bands
    freqs = width_cols // bands
    table = jnp.asarray(column_table(width_cols, bands))
    stacked = jnp.concatenate([coeff_maps, image], axis=0)
    send = jnp.einsum("mrn,bnk->brmk", stacked, table, preferred_element_type=f32)
    got = lax.all_to_all(send.astype(bf16), "band", split_axis=0, concat_axis=0)
    got = got.reshape(height, filters + channels, 2, freqs)
    ramp = jnp.arange(height, dtype=jnp.int32)
    angles = (ramp[:, None] * ramp[None, :] % height).astype(f32) * (2.0 * math.pi / height)
    factor = 1.0 / math.sqrt(height)
    lookup = jnp.stack([jnp.cos(angles) * factor, jnp.sin(angles) * factor]).astype(bf16)
    both = jnp.einsum("hmpq,tgh->ptqmg", got, lookup, preferred_element_type=f32)
    re = both[0, 0] + both[1, 1]
    im = both[1, 0] - both[0, 1]
    x_re, s_re = re[:, :filters], re[:, filters:]
    x_im, s_im = im[:, :filters], im[:, filters:]
    v_re = target[:, 0].astype(f32)
    v_im = target[:, 1].astype(f32)
    energy = jnp.sum(x_re * x_re + x_im * x_im, axis=1)
    cross_re = jnp.sum(x_re[:, None] * v_re - x_im[:, None] * v_im, axis=2)
    cross_im = jnp.sum(x_re[:, None] * v_im + x_im[:, None] * v_re, axis=2)
    sums = jnp.concatenate([cross_re, cross_im, energy[:, None]], axis=1)
    sums = lax.psum(sums.astype(bf16), "filt").astype(f32)
    denom = penalty + sums[:, 2 * channels :]
    coef_re = ((s_re - sums[:, :channels]) / denom)[:, :, None]
    coef_im = ((s_im - sums[:, channels : 2 * channels]) / denom)[:, :, None]
    d_re = v_re + x_re[:, None] * coef_re + x_im[:, None] * coef_im
    d_im = v_im + x_re[:, None] * coef_im - x_im[:, None] * coef_re
    reach = jnp.arange(K, dtype=jnp.int32)
    rows = (ramp[:, None] * reach[None, :] % height).astype(f32) * (2.0 * math.pi / height)
    cols = lax.axis_index("band") * freqs + jnp.arange(freqs, dtype=jnp.int32)
    cols = (cols[:, None] * reach[None, :] % width_cols).astype(f32) * (2.0 * math.pi / width_cols)
    turn = rows[None, :, :, None] + cols[:, None, None, :]
    factor = 1.0 / math.sqrt(height * width_cols)
    exact = lax.Precision.HIGHEST
    spatial = jnp.einsum("qcmg,qgyx->mcyx", d_re, jnp.cos(turn) * factor, precision=exact)
    spatial -= jnp.einsum("qcmg,qgyx->mcyx", d_im, jnp.sin(turn) * factor, precision=exact)
    spatial = lax.psum(spatial.reshape(dual_rim.shape), "band")
    joined = spatial + dual_rim
    spread = jnp.sqrt(jnp.mean(joined * joined, axis=1, keepdims=True))
    dict_spectra = jnp.stack([d_re, d_im], axis=1).astype(bf16)
    return (dict_spectra, joined / jnp.maximum(spread, 1.0))


def body(coeff_maps, image, target, dual_rim):
    filters, band_rows, width_cols = coeff_maps.shape
    channels = image.shape[0]
    bands = lax.axis_size("band")
    height = band_rows * bands
    freqs = width_cols // bands
    rows = (filters + channels - 1) * band_rows
    cores = lax.axis_size("filt")
    fits = (2 * freqs, 2 * height, band_rows, channels, filters % 2, bands & (bands - 1), cores)
    if fits != (LANES, LANES, 8, 3, 0, 0, 2):
        return plain(coeff_maps, image, target, dual_rim)

    def swap(array, k):
        return lax.ppermute(array, "band", [(i, i ^ k) for i in range(bands)])

    lines, table = pl.pallas_call(
        fetch_kernel,
        out_shape=(
            jax.ShapeDtypeStruct((rows, width_cols), bf16),
            jax.ShapeDtypeStruct((width_cols, bands // 2 * LANES), bf16),
        ),
        in_specs=[pl.BlockSpec(memory_space=pltpu.HBM)] * 3,
        scratch_shapes=[pltpu.SemaphoreType.DMA((2,)), pltpu.SemaphoreType.DMA((bands // 2,))],
        compiler_params=params(8),
        name="fetch",
    )(
        far(coeff_maps.reshape(filters * band_rows, width_cols)),
        far(image.reshape(channels * band_rows, width_cols)),
        far(jnp.asarray(column_table(width_cols, bands)[: bands // 2])),
    )
    chunks = pl.pallas_call(
        columns_kernel,
        out_shape=(jax.ShapeDtypeStruct((rows, LANES), bf16),) * bands,
        compiler_params=params(8),
        name="columns",
    )(lines, table)
    got = [swap(chunks[k], k) if k else chunks[k] for k in far_first(bands)]

    turns = turn_table(width_cols, K, GROUP).reshape(bands, freqs // GROUP, 2 * K * K)
    packed = pl.pallas_call(
        prepare_kernel,
        out_shape=jax.ShapeDtypeStruct((freqs, channels, filters, LANES), f32),
        in_specs=[pl.BlockSpec(memory_space=pltpu.HBM)],
        scratch_shapes=[pltpu.VMEM(target.shape, bf16), pltpu.SemaphoreType.DMA((CHUNKS,))],
        compiler_params=params(12),
        name="prepare",
    )(far(target))

    lines = (channels + 1) * freqs
    x, own, sums = pl.pallas_call(
        rows_kernel,
        out_shape=(
            jax.ShapeDtypeStruct((freqs * filters, LANES), f32),
            jax.ShapeDtypeStruct((lines, LANES), f32),
            jax.ShapeDtypeStruct((lines, LANES), bf16),
        ),
        scratch_shapes=[
            pltpu.VMEM((lines, LANES), f32),
            pltpu.VMEM((channels * freqs, LANES), f32),
            pltpu.VMEM((channels * freqs, LANES), f32),
            pltpu.VMEM(((filters // 2 + channels - 2) * freqs, 2 * LANES), bf16),
        ],
        compiler_params=params(8),
        name="rows",
    )(*got, jnp.asarray(row_table(height, band_rows)), packed)

    peer = lax.ppermute(sums, "filt", [(0, 1), (1, 0)])

    held, rim = pl.pallas_call(
        solve_kernel,
        out_shape=(
            jax.ShapeDtypeStruct(target.shape, bf16),
            jax.ShapeDtypeStruct((channels * filters, K * K), bf16),
        ),
        scratch_shapes=[
            pltpu.VMEM((channels * freqs, LANES), f32),
            pltpu.VMEM((channels * freqs, LANES), f32),
        ],
        compiler_params=params(16),
        name="solve",
    )(x, packed, own, peer, jnp.asarray(inverse_table(height, width_cols, K, GROUP)), jnp.asarray(turns))

    dict_spectra = pl.pallas_call(
        write_kernel,
        out_shape=jax.ShapeDtypeStruct(target.shape, bf16),
        in_specs=[pl.BlockSpec(memory_space=pltpu.VMEM)],
        out_specs=pl.BlockSpec(memory_space=pltpu.HBM),
        scratch_shapes=[pltpu.SemaphoreType.DMA],
        compiler_params=params(4),
        name="write",
    )(held)

    near = swap(rim, 1)
    pair = pl.pallas_call(
        add_kernel,
        out_shape=jax.ShapeDtypeStruct(rim.shape, bf16),
        compiler_params=params(4),
        name="add",
    )(rim, near)
    parts = [pair] + [swap(pair, k) for k in (4, 2, 6)]
    dictionary = pl.pallas_call(
        finish_kernel,
        out_shape=jax.ShapeDtypeStruct(dual_rim.shape, f32),
        compiler_params=params(4),
        name="finish",
    )(*parts, dual_rim)
    return (dict_spectra, dictionary)


def solution(mesh):
    placed = (
        P(("grp", "filt"), "band", None),
        P("grp", "band", None),
        P(("grp", "band"), None, None, "filt", None),
        P(("grp", "filt"), None),
    )
    return jax.shard_map(
        body,
        mesh=mesh,
        in_specs=placed,
        out_specs=(P(("grp", "band"), None, None, "filt", None), P(("grp", "filt"), None)),
        check_vma=False,
    )
```
